256 devices in a mesh: blk: 32 (over x_lo, z, core), slab: 8 (over x_hi, y).
Axes of the slice: x: 4 (x_hi: 2, x_lo: 2; x = x_hi * 2 + x_lo), y: 4, z: 8, core: 2. Of those that a mesh axis runs over, the one named last changes fastest.
Arguments:
- tokens: bfloat16 [4194304, 128], P(('blk', 'slab')), may hold values from -6 to 6
- listed: int32 [16384, 3], P(('blk', 'slab')), may hold values from 0 to 1023, as said below
- centroids: bfloat16 [262144, 128], P('blk'), may hold values from -6 to 6
Outputs:
- refined: float32 [262144, 128], P(('blk', 'slab'))
- counts: float32 [262144], P(('blk', 'slab'))
The draws below stay inside these ranges and needn't reach their ends.
Inputs may be any that keep to these rules, and one draw needn't show every extreme that they name: `listed`: in the rows of one device (64 token blocks), all ids of one owner group (id // 32) are equal, so a device names at most one block of each owner group. The three ids of a row are distinct.
All inputs are finite; a program needn't handle non-finite values.
Results may differ from the reference program's by a relative error of at most 0.00093.
Values may be sent and summed in bfloat16 or wider, within the bound.
No kernel may reach another device: no remote copies, remote signals or barrier semaphores. Data moves between devices by JAX's collectives and lax.ppermute only.
A program may use at most 128 MiB of HBM per device.

```python
import jax
import jax.numpy as jnp
from jax import lax

EMBED_WIDTH = 128
CENT_BLK = 256
TOK_BLK = 256
BPO = 32
TBD = 64
USED = 24
CENTROIDS = 262144
TOKENS = 4194304
N_BLK = 32
N_SLAB = 8


def draw_listed(key, part):
    device_count = N_BLK * N_SLAB
    hot_key = jax.random.fold_in(key, 11)
    label_key = jax.random.fold_in(key, 12)
    within_key = jax.random.fold_in(key, 13)
    pick_key = jax.random.fold_in(key, 14)
    hot_owner = jax.random.randint(hot_key, (N_SLAB,), 0, N_BLK)
    device_keys = jax.random.split(label_key, device_count)
    other_labels = jax.vmap(lambda row_key: jax.random.permutation(row_key, N_BLK - 1)[:USED - 1] + 1)(device_keys)
    owner_labels = jnp.concatenate([jnp.zeros((device_count, 1), jnp.int32), other_labels.astype(jnp.int32)], axis=1)
    slab_of = jnp.arange(device_count, dtype=jnp.int32) % N_SLAB
    owner_lookup = (owner_labels + hot_owner[slab_of][:, None]) % N_BLK
    within_ids = jax.random.randint(within_key, (device_count, USED), 0, BPO)
    block_table = owner_lookup * BPO + within_ids
    row_keys = jax.random.split(pick_key, device_count * TBD)
    picked_slots = jax.vmap(lambda row_key: jax.random.permutation(row_key, USED)[:3])(row_keys)
    device_of = jnp.arange(device_count * TBD, dtype=jnp.int32) // TBD
    chosen = block_table[device_of[:, None], picked_slots]
    return chosen.astype(jnp.int32)


def block_levels(rng, extent, shards, smallest, high):
    def one(axis_at, blocks):
        heights = jax.random.uniform(jax.random.fold_in(jax.random.fold_in(rng, 6), axis_at), (blocks,), jnp.float32, smallest / len(shards), high / len(shards))
        return jnp.repeat(jnp.exp(heights), extent[axis_at] // blocks).reshape((-1,) + (1,) * (len(extent) - axis_at - 1))

    gain = one(*shards[0])
    for cut in shards[1:]:
        gain = gain * one(*cut)
    return gain


def gaussian(stream_key, extent, scale, most, pieces=(), held_as=jnp.bfloat16):
    drawn = scale * jax.random.normal(stream_key, extent, jnp.float32)
    if pieces:
        drawn = drawn * block_levels(stream_key, extent, pieces, -0.22, 0.18)
    return jnp.clip(drawn, -most, most).astype(held_as)


def setup_inputs(seed: int = 0) -> dict:
    keys = jax.random.split(jax.random.key(seed), 4)
    return {
        "tokens": gaussian(keys[0], (TOKENS, EMBED_WIDTH), 1.0, 6.0, ((0, 256),)),
        "listed": draw_listed(jax.random.fold_in(keys[3], 71), 0),
        "centroids": gaussian(keys[2], (CENTROIDS, EMBED_WIDTH), 1.0, 6.0, ((0, 32),)),
    }


SOFTMAX_TEMP = 0.1
PRIOR_WEIGHT = 4.0
EPSILON = 1e-06

def unit_rows(values):
    widened = values.astype(jnp.float32)
    return widened * lax.rsqrt(lax.optimization_barrier(jnp.mean(widened * widened, axis=-1, keepdims=True)) + EPSILON)

def reference(tokens, listed, centroids):
    centroid_norm = unit_rows(centroids)
    cent_round = lax.optimization_barrier(centroid_norm.astype(jnp.bfloat16))
    cent_round = cent_round.astype(jnp.float32).reshape(-1, CENT_BLK, EMBED_WIDTH)
    tok_round = lax.optimization_barrier(unit_rows(tokens).astype(jnp.bfloat16))
    tok_round = tok_round.astype(jnp.float32).reshape(-1, TOK_BLK, EMBED_WIDTH)
    nblocks = listed.shape[0]
    batch = 32
    total_blocks = cent_round.shape[0]

    def accumulate(state_pair, turn_index):
        sum_acc, count_acc = state_pair
        start = (turn_index * batch).astype(jnp.int32)
        token_rows = lax.dynamic_slice_in_dim(tok_round, start, batch, 0)
        block_ids = lax.dynamic_slice_in_dim(listed, start, batch, 0)
        candidate_centroids = cent_round[block_ids].reshape(batch, 3 * CENT_BLK, EMBED_WIDTH)
        score_matrix = jnp.einsum('wsy,way->wsa', token_rows, candidate_centroids) / (EMBED_WIDTH * SOFTMAX_TEMP)
        weights = jnp.exp(score_matrix)
        weights = weights / lax.optimization_barrier(jnp.sum(weights, axis=-1, keepdims=True))
        weights_low = lax.optimization_barrier(weights.astype(jnp.bfloat16)).astype(jnp.float32)
        weights_low = weights_low.reshape(batch, TOK_BLK, 3, CENT_BLK)
        partial_value = jnp.einsum('gtkc,gtd->gkcd', weights_low, token_rows)
        part_counts = lax.optimization_barrier(jnp.sum(weights.reshape(batch, TOK_BLK, 3, CENT_BLK), axis=1))
        flat_ids = block_ids.reshape(-1)
        sum_acc = sum_acc.at[flat_ids].add(partial_value.reshape(-1, CENT_BLK, EMBED_WIDTH))
        count_acc = count_acc.at[flat_ids].add(part_counts.reshape(-1, CENT_BLK))
        return ((sum_acc, count_acc), None)
    start_pair = (jnp.zeros((total_blocks, CENT_BLK, EMBED_WIDTH), jnp.float32), jnp.zeros((total_blocks, CENT_BLK), jnp.float32))
    (sum_acc, count_acc), _ = lax.scan(accumulate, start_pair, jnp.arange(nblocks // batch, dtype=jnp.int32))
    sum_flat = sum_acc.reshape(-1, EMBED_WIDTH)
    count_flat = count_acc.reshape(-1)
    refined = (sum_flat + PRIOR_WEIGHT * centroid_norm) / (count_flat[:, None] + PRIOR_WEIGHT)
    return (refined, count_flat)
```

```python
import functools
import math

import jax
import jax.numpy as jnp
from jax import lax
from jax.experimental import pallas as pl
from jax.experimental.pallas import tpu as pltpu
from jax.sharding import PartitionSpec as P

EMBED_WIDTH = 128
CENT_BLK = 256
TOK_BLK = 256
BPO = 32
MSG_ROWS = CENT_BLK + 8

SOFTMAX_TEMP = 0.1
PRIOR_WEIGHT = 4.0
EPSILON = 1e-06
EXP2_SCALE = math.log2(math.e) / (EMBED_WIDTH * SOFTMAX_TEMP)
CONTRACT_LAST = (((1,), (1,)), ((), ()))


def unit_rows(values):
    widened = values.astype(jnp.float32)
    return widened * lax.rsqrt(jnp.mean(widened * widened, axis=-1, keepdims=True) + EPSILON)


def split_counts(totals_a, totals_b):
    row = lax.broadcasted_iota(jnp.int32, (8, EMBED_WIDTH), 0)
    heads = jnp.where(row % 2 == 0, totals_a, totals_b)
    rounded = heads.astype(jnp.bfloat16).astype(jnp.float32)
    tails = heads - rounded
    tile = jnp.where(row < 2, rounded, jnp.where(row < 4, tails, 0.0))
    return tile.astype(jnp.bfloat16)


def attend_kernel(per_step, slots, tok_ref, cent_ref, out_ref, acc_ref, cnt_ref):
    step = pl.program_id(0)

    @pl.when(step == 0)
    def _():
        acc_ref[...] = jnp.zeros_like(acc_ref)
        cnt_ref[...] = jnp.zeros_like(cnt_ref)

    for at in range(per_step):
        block = step * per_step + at
        tok = unit_rows(tok_ref[pl.ds(at * TOK_BLK, TOK_BLK), :]).astype(jnp.bfloat16)
        ids = [slots[block * 3 + k] for k in range(3)]
        exps = []
        total = None
        for k in range(3):
            scores = lax.dot_general(
                cent_ref[ids[k]], tok, CONTRACT_LAST, preferred_element_type=jnp.float32
            )
            grown = jnp.exp2(scores * EXP2_SCALE)
            exps.append(grown)
            part = jnp.sum(grown, axis=0, keepdims=True)
            total = part if total is None else total + part
        inverse = 1.0 / total
        for k in range(3):
            weights = exps[k] * inverse
            cnt_ref[ids[k]] += weights[:, :128] + weights[:, 128:]
            acc_ref[ids[k]] += jnp.dot(
                weights.astype(jnp.bfloat16), tok, preferred_element_type=jnp.float32
            )

    @pl.when(step == pl.num_programs(0) - 1)
    def _():
        ones = jnp.ones((8, EMBED_WIDTH), jnp.float32)

        def write(slot, carry):
            out_ref[slot, :CENT_BLK, :] = acc_ref[slot].astype(jnp.bfloat16)
            counts = lax.dot_general(
                ones, cnt_ref[slot], CONTRACT_LAST,
                preferred_element_type=jnp.float32, precision=lax.Precision.HIGHEST,
            )
            out_ref[slot, CENT_BLK:, :] = split_counts(counts[:, :128], counts[:, 128:])
            return carry

        lax.fori_loop(0, cnt_ref.shape[0], write, 0)


def attend(slots, tokens, fetched, per_step=4):
    owners = fetched.shape[0]
    blocks = tokens.shape[0] // TOK_BLK
    per_step = math.gcd(per_step, blocks)
    pairs = blocks * 3 * TOK_BLK * CENT_BLK
    return pl.pallas_call(
        functools.partial(attend_kernel, per_step),
        grid_spec=pltpu.PrefetchScalarGridSpec(
            num_scalar_prefetch=1,
            grid=(blocks // per_step,),
            in_specs=[
                pl.BlockSpec((per_step * TOK_BLK, EMBED_WIDTH), lambda i, s: (i, 0)),
                pl.BlockSpec(fetched.shape, lambda i, s: (0, 0, 0), pipeline_mode=pl.Buffered(1)),
            ],
            out_specs=pl.BlockSpec(
                (owners, MSG_ROWS, EMBED_WIDTH), lambda i, s: (0, 0, 0),
                pipeline_mode=pl.Buffered(1),
            ),
            scratch_shapes=[
                pltpu.VMEM((owners, CENT_BLK, EMBED_WIDTH), jnp.float32),
                pltpu.VMEM((owners, CENT_BLK, EMBED_WIDTH), jnp.float32),
            ],
        ),
        out_shape=jax.ShapeDtypeStruct((owners, MSG_ROWS, EMBED_WIDTH), jnp.bfloat16),
        compiler_params=pltpu.CompilerParams(vmem_limit_bytes=40 << 20),
        cost_estimate=pl.CostEstimate(
            flops=pairs * EMBED_WIDTH * 4, transcendentals=pairs,
            bytes_accessed=tokens.size * 2 + fetched.size * 4,
        ),
        name="attend",
    )(slots, tokens, fetched)


def collect_kernel(asked, back_ref, out_ref, acc_ref):
    acc_ref[...] = jnp.zeros_like(acc_ref)

    def add(source, carry):
        inner = asked[source]

        @pl.when(inner >= 0)
        def _():
            acc_ref[inner] += back_ref[source].astype(jnp.float32)

        return carry

    lax.fori_loop(0, back_ref.shape[0], add, 0)

    def write(inner, carry):
        out_ref[inner, :CENT_BLK, :] = acc_ref[inner, :CENT_BLK, :].astype(jnp.bfloat16)
        tile = acc_ref[inner, CENT_BLK:, :]
        totals = tile[0:2] + tile[2:4]
        out_ref[inner, CENT_BLK:, :] = split_counts(totals[0:1], totals[1:2])
        return carry

    lax.fori_loop(0, out_ref.shape[0], write, 0)


def collect(asked, back):
    shape = (BPO, MSG_ROWS, EMBED_WIDTH)
    return pl.pallas_call(
        collect_kernel,
        grid_spec=pltpu.PrefetchScalarGridSpec(
            num_scalar_prefetch=1,
            grid=(1,),
            in_specs=[pl.BlockSpec(back.shape, lambda i, s: (0, 0, 0), pipeline_mode=pl.Buffered(1))],
            out_specs=pl.BlockSpec(shape, lambda i, s: (0, 0, 0), pipeline_mode=pl.Buffered(1)),
            scratch_shapes=[pltpu.VMEM(shape, jnp.float32)],
        ),
        out_shape=jax.ShapeDtypeStruct(shape, jnp.bfloat16),
        compiler_params=pltpu.CompilerParams(vmem_limit_bytes=24 << 20),
        cost_estimate=pl.CostEstimate(
            flops=back.size, transcendentals=0, bytes_accessed=back.size * 4
        ),
        name="collect",
    )(asked, back)


def shards(tokens, listed, centroids):
    owner_count = lax.axis_size("blk")
    slab_count = lax.axis_size("slab")
    slab_index = lax.axis_index("slab")
    share_blocks = BPO // slab_count

    owner_ids = jnp.arange(owner_count, dtype=jnp.int32)
    group_of = listed // BPO
    inner_ids = listed % BPO
    matches = group_of[:, :, None] == owner_ids
    wanted = jnp.max(jnp.where(matches, inner_ids[:, :, None] + 1, 0), axis=(0, 1)) - 1
    asked_ids = lax.all_to_all(
        wanted.reshape(owner_count, 1), "blk", split_axis=0, concat_axis=0, tiled=True
    ).reshape(owner_count)

    cent_send = unit_rows(centroids).astype(jnp.bfloat16).reshape(BPO, CENT_BLK, EMBED_WIDTH)
    replies = cent_send[jnp.maximum(asked_ids, 0)]
    fetched = lax.all_to_all(replies, "blk", split_axis=0, concat_axis=0, tiled=True)

    partial = attend(group_of.reshape(-1), tokens, fetched)
    back = lax.all_to_all(partial, "blk", split_axis=0, concat_axis=0, tiled=True)
    own = collect(asked_ids, back)
    slabs = lax.all_to_all(own, "slab", split_axis=0, concat_axis=0, tiled=True)
    slabs = slabs.reshape(slab_count, share_blocks, MSG_ROWS, EMBED_WIDTH)

    totals = jnp.sum(slabs.astype(jnp.float32), axis=0)
    counts = (totals[:, CENT_BLK:CENT_BLK + 2] + totals[:, CENT_BLK + 2:CENT_BLK + 4]).reshape(-1)
    sums = totals[:, :CENT_BLK].reshape(-1, EMBED_WIDTH)
    rows = share_blocks * CENT_BLK
    mine = unit_rows(lax.dynamic_slice_in_dim(centroids, slab_index * rows, rows, 0))
    refined = (sums + PRIOR_WEIGHT * mine) / (counts[:, None] + PRIOR_WEIGHT)
    return refined, counts


def solution(mesh):
    placed = (P(("blk", "slab"), None), P(("blk", "slab"), None), P("blk", None))
    return jax.shard_map(
        shards,
        mesh=mesh,
        in_specs=placed,
        out_specs=(P(("blk", "slab"), None), P(("blk", "slab"))),
        check_vma=False,
    )
```

```python
import functools
import math

import jax
import jax.numpy as jnp
from jax import lax
from jax.experimental import pallas as pl
from jax.experimental.pallas import tpu as pltpu
from jax.sharding import PartitionSpec as P

EMBED_WIDTH = 128
CENT_BLK = 256
TOK_BLK = 256
BPO = 32
MSG_ROWS = CENT_BLK + 8

SOFTMAX_TEMP = 0.1
PRIOR_WEIGHT = 4.0
EPSILON = 1e-06
EXP2_SCALE = math.log2(math.e) / (EMBED_WIDTH * SOFTMAX_TEMP)
CONTRACT_LAST = (((1,), (1,)), ((), ()))


def unit_rows(values):
    widened = values.astype(jnp.float32)
    return widened * lax.rsqrt(jnp.mean(widened * widened, axis=-1, keepdims=True) + EPSILON)


def split_counts(totals_a, totals_b):
    row = lax.broadcasted_iota(jnp.int32, (8, EMBED_WIDTH), 0)
    heads = jnp.where(row % 2 == 0, totals_a, totals_b)
    rounded = heads.astype(jnp.bfloat16).astype(jnp.float32)
    tails = heads - rounded
    tile = jnp.where(row < 2, rounded, jnp.where(row < 4, tails, 0.0))
    return tile.astype(jnp.bfloat16)


def attend_kernel(per_step, unroll, slots, tok_ref, cent_ref, out_ref, acc_ref, cnt_ref, exp_ref, inv_ref, unit_ref, turned_ref):
    step = pl.program_id(0)

    @pl.when(step == 0)
    def _():
        acc_ref[...] = jnp.zeros_like(acc_ref)
        cnt_ref[...] = jnp.zeros_like(cnt_ref)
        exp_ref[1] = jnp.zeros(exp_ref.shape[1:], exp_ref.dtype)
        inv_ref[1] = jnp.zeros(inv_ref.shape[1:], inv_ref.dtype)
        turned_ref[3] = jnp.zeros(turned_ref.shape[1:], turned_ref.dtype)

    def spread(block, side):
        inverse = inv_ref[side % 2]

        def piece(k):
            slot = slots[block * 3 + k]
            left = exp_ref[side % 2, k, :, :128] * inverse
            right = exp_ref[side % 2, k, :, 128:] * inverse
            weights = jnp.concatenate([left, right], axis=1)
            cnt_ref[slot] += jnp.sum(weights.reshape(TOK_BLK // 8, 8, CENT_BLK), axis=0)
            acc_ref[slot] += jnp.dot(
                turned_ref[side], weights.astype(jnp.bfloat16), preferred_element_type=jnp.float32
            )

        return piece

    def prepare(at, side):
        rows = pl.ds(pl.multiple_of(at * TOK_BLK, TOK_BLK), TOK_BLK)
        tok = unit_rows(tok_ref[rows, :]).astype(jnp.bfloat16)
        unit_ref[side] = tok
        turned_ref[side] = tok.T

    def score(block, side):
        totals = []

        def piece(k):
            slot = slots[block * 3 + k]
            scores = jnp.dot(unit_ref[side], cent_ref[slot], preferred_element_type=jnp.float32)
            grown = jnp.exp2(scores * EXP2_SCALE)
            exp_ref[side % 2, k] = grown
            part = grown[:, :128] + grown[:, 128:]
            totals.append(part if not totals else totals.pop() + part)

        def close():
            total = jnp.sum(totals[0], axis=1, keepdims=True)
            inv_ref[side % 2] = jnp.broadcast_to(1.0 / total, inv_ref.shape[1:])

        return piece, close

    def both(at, u):
        block = step * per_step + at
        piece_a, close = score(block, u % 4)
        piece_b = spread(jnp.maximum(block - 1, 0), (u - 1) % 4)
        prepare(jnp.minimum(at + 1, per_step - 1), (u + 1) % 4)
        for k in range(3):
            piece_a(k)
            piece_b(k)
        close()

    def pair(index, carry):
        for u in range(unroll):
            both(unroll * index + u, u)
        return carry

    prepare(0, 0)
    lax.fori_loop(0, per_step // unroll, pair, 0)

    @pl.when(step == pl.num_programs(0) - 1)
    def _():
        piece = spread(pl.num_programs(0) * per_step - 1, 3)
        for k in range(3):
            piece(k)
        finish(out_ref, acc_ref, cnt_ref)


def finish(out_ref, acc_ref, cnt_ref):
    def write(slot, carry):
        out_ref[slot, :128, :] = acc_ref[slot, :, :128].astype(jnp.bfloat16)
        out_ref[slot, 128:256, :] = acc_ref[slot, :, 128:].astype(jnp.bfloat16)
        counts = jnp.sum(cnt_ref[slot], axis=0, keepdims=True)
        out_ref[slot, CENT_BLK:, :] = split_counts(counts[:, :128], counts[:, 128:])
        return carry

    lax.fori_loop(0, cnt_ref.shape[0], write, 0, unroll=4)


def attend(slots, tokens, fetched, per_step=64, unroll=4):
    owners = fetched.shape[0]
    blocks = tokens.shape[0] // TOK_BLK
    per_step = math.gcd(per_step, blocks)
    pairs = blocks * 3 * TOK_BLK * CENT_BLK
    return pl.pallas_call(
        functools.partial(attend_kernel, per_step, unroll),
        grid_spec=pltpu.PrefetchScalarGridSpec(
            num_scalar_prefetch=1,
            grid=(blocks // per_step,),
            in_specs=[
                pl.BlockSpec((per_step * TOK_BLK, EMBED_WIDTH), lambda i, s: (i, 0)),
                pl.BlockSpec(fetched.shape, lambda i, s: (0, 0, 0), pipeline_mode=pl.Buffered(1)),
            ],
            out_specs=pl.BlockSpec(
                (owners, MSG_ROWS, EMBED_WIDTH), lambda i, s: (0, 0, 0),
                pipeline_mode=pl.Buffered(1),
            ),
            scratch_shapes=[
                pltpu.VMEM((owners, EMBED_WIDTH, CENT_BLK), jnp.float32),
                pltpu.VMEM((owners, 8, CENT_BLK), jnp.float32),
                pltpu.VMEM((2, 3, TOK_BLK, CENT_BLK), jnp.float32),
                pltpu.VMEM((2, TOK_BLK, 128), jnp.float32),
                pltpu.VMEM((4, TOK_BLK, EMBED_WIDTH), jnp.bfloat16),
                pltpu.VMEM((4, EMBED_WIDTH, TOK_BLK), jnp.bfloat16),
            ],
        ),
        out_shape=jax.ShapeDtypeStruct((owners, MSG_ROWS, EMBED_WIDTH), jnp.bfloat16),
        compiler_params=pltpu.CompilerParams(vmem_limit_bytes=40 << 20),
        cost_estimate=pl.CostEstimate(
            flops=pairs * EMBED_WIDTH * 4, transcendentals=pairs,
            bytes_accessed=tokens.size * 2 + fetched.size * 4,
        ),
        name="attend",
    )(slots, tokens, fetched)


def collect_kernel(asked, back_ref, out_ref, acc_ref):
    acc_ref[...] = jnp.zeros_like(acc_ref)

    def add(source, carry):
        inner = asked[source]

        @pl.when(inner >= 0)
        def _():
            acc_ref[inner] += back_ref[source].astype(jnp.float32)

        return carry

    lax.fori_loop(0, back_ref.shape[0], add, 0)

    def write(inner, carry):
        out_ref[inner, :CENT_BLK, :] = acc_ref[inner, :CENT_BLK, :].astype(jnp.bfloat16)
        tile = acc_ref[inner, CENT_BLK:, :]
        totals = tile[0:2] + tile[2:4]
        out_ref[inner, CENT_BLK:, :] = split_counts(totals[0:1], totals[1:2])
        return carry

    lax.fori_loop(0, out_ref.shape[0], write, 0)


def collect(asked, back):
    shape = (BPO, MSG_ROWS, EMBED_WIDTH)
    return pl.pallas_call(
        collect_kernel,
        grid_spec=pltpu.PrefetchScalarGridSpec(
            num_scalar_prefetch=1,
            grid=(1,),
            in_specs=[pl.BlockSpec(back.shape, lambda i, s: (0, 0, 0), pipeline_mode=pl.Buffered(1))],
            out_specs=pl.BlockSpec(shape, lambda i, s: (0, 0, 0), pipeline_mode=pl.Buffered(1)),
            scratch_shapes=[pltpu.VMEM(shape, jnp.float32)],
        ),
        out_shape=jax.ShapeDtypeStruct(shape, jnp.bfloat16),
        compiler_params=pltpu.CompilerParams(vmem_limit_bytes=24 << 20),
        cost_estimate=pl.CostEstimate(
            flops=back.size, transcendentals=0, bytes_accessed=back.size * 4
        ),
        name="collect",
    )(asked, back)


def shards(tokens, listed, centroids):
    owner_count = lax.axis_size("blk")
    slab_count = lax.axis_size("slab")
    slab_index = lax.axis_index("slab")
    share_blocks = BPO // slab_count

    owner_ids = jnp.arange(owner_count, dtype=jnp.int32)
    group_of = listed // BPO
    inner_ids = listed % BPO
    matches = group_of[:, :, None] == owner_ids
    wanted = jnp.max(jnp.where(matches, inner_ids[:, :, None] + 1, 0), axis=(0, 1)) - 1
    asked_ids = lax.all_to_all(
        wanted.reshape(owner_count, 1), "blk", split_axis=0, concat_axis=0, tiled=True
    ).reshape(owner_count)

    cent_send = unit_rows(centroids).astype(jnp.bfloat16).reshape(BPO, CENT_BLK, EMBED_WIDTH)
    cent_send = cent_send.transpose(0, 2, 1)
    replies = cent_send[jnp.maximum(asked_ids, 0)]
    fetched = lax.all_to_all(replies, "blk", split_axis=0, concat_axis=0, tiled=True)

    partial = attend(group_of.reshape(-1), tokens, fetched)
    back = lax.all_to_all(partial, "blk", split_axis=0, concat_axis=0, tiled=True)
    own = collect(asked_ids, back)
    slabs = lax.all_to_all(own, "slab", split_axis=0, concat_axis=0, tiled=True)
    slabs = slabs.reshape(slab_count, share_blocks, MSG_ROWS, EMBED_WIDTH)

    totals = jnp.sum(slabs.astype(jnp.float32), axis=0)
    counts = (totals[:, CENT_BLK:CENT_BLK + 2] + totals[:, CENT_BLK + 2:CENT_BLK + 4]).reshape(-1)
    halves = totals[:, :CENT_BLK].reshape(share_blocks, 2, EMBED_WIDTH, CENT_BLK // 2)
    sums = halves.transpose(0, 1, 3, 2).reshape(-1, EMBED_WIDTH)
    rows = share_blocks * CENT_BLK
    mine = unit_rows(lax.dynamic_slice_in_dim(centroids, slab_index * rows, rows, 0))
    refined = (sums + PRIOR_WEIGHT * mine) / (counts[:, None] + PRIOR_WEIGHT)
    return refined, counts


def solution(mesh):
    placed = (P(("blk", "slab"), None), P(("blk", "slab"), None), P("blk", None))
    return jax.shard_map(
        shards,
        mesh=mesh,
        in_specs=placed,
        out_specs=(P(("blk", "slab"), None), P(("blk", "slab"))),
        check_vma=False,
    )
```

```python
import functools
import math

import jax
import jax.numpy as jnp
from jax import lax
from jax.experimental import pallas as pl
from jax.experimental.pallas import tpu as pltpu
from jax.sharding import Mesh
from jax.sharding import PartitionSpec as P

EMBED_WIDTH = 128
CENT_BLK = 256
TOK_BLK = 256
BPO = 32
MSG_ROWS = CENT_BLK + 8

SOFTMAX_TEMP = 0.1
PRIOR_WEIGHT = 4.0
EPSILON = 1e-06
EXP2_SCALE = math.log2(math.e) / (EMBED_WIDTH * SOFTMAX_TEMP)
CONTRACT_LAST = (((1,), (1,)), ((), ()))


def unit_rows(values):
    widened = values.astype(jnp.float32)
    return widened * lax.rsqrt(jnp.mean(widened * widened, axis=-1, keepdims=True) + EPSILON)


def split_counts(totals_a, totals_b):
    row = lax.broadcasted_iota(jnp.int32, (8, EMBED_WIDTH), 0)
    heads = jnp.where(row % 2 == 0, totals_a, totals_b)
    rounded = heads.astype(jnp.bfloat16).astype(jnp.float32)
    tails = heads - rounded
    tile = jnp.where(row < 2, rounded, jnp.where(row < 4, tails, 0.0))
    return tile.astype(jnp.bfloat16)


def prepare_kernel(tok_ref, unit_ref, turned_ref):
    tok = unit_rows(tok_ref[...]).astype(jnp.bfloat16)
    unit_ref[...] = tok
    for at in range(turned_ref.shape[0]):
        turned_ref[at] = tok[at * TOK_BLK:(at + 1) * TOK_BLK].T


def prepare(tokens, per_step=4):
    blocks = tokens.shape[0] // TOK_BLK
    per_step = math.gcd(per_step, blocks)
    rows = per_step * TOK_BLK
    return pl.pallas_call(
        prepare_kernel,
        grid=(blocks // per_step,),
        in_specs=[pl.BlockSpec((rows, EMBED_WIDTH), lambda i: (i, 0))],
        out_specs=(
            pl.BlockSpec((rows, EMBED_WIDTH), lambda i: (i, 0)),
            pl.BlockSpec((per_step, EMBED_WIDTH, TOK_BLK), lambda i: (i, 0, 0)),
        ),
        out_shape=(
            jax.ShapeDtypeStruct(tokens.shape, jnp.bfloat16),
            jax.ShapeDtypeStruct((blocks, EMBED_WIDTH, TOK_BLK), jnp.bfloat16),
        ),
        compiler_params=pltpu.CompilerParams(vmem_limit_bytes=8 << 20),
        cost_estimate=pl.CostEstimate(
            flops=tokens.size * 4, transcendentals=tokens.shape[0], bytes_accessed=tokens.size * 6
        ),
        name="prepare",
    )(tokens)


def attend_kernel(unroll, slots, ids, unit_ref, turned_ref, recv_ref, out_ref, acc_ref, cnt_ref, exp_ref, inv_ref, cent_ref):
    blocks = turned_ref.shape[0]
    acc_ref[...] = jnp.zeros_like(acc_ref)
    cnt_ref[...] = jnp.zeros_like(cnt_ref)
    exp_ref[1] = jnp.zeros(exp_ref.shape[1:], exp_ref.dtype)
    inv_ref[1] = jnp.zeros(inv_ref.shape[1:], inv_ref.dtype)
    quads, slabs, depth = recv_ref.shape[:3]
    cores = 2
    for quad in range(quads):
        def turn(at, carry):
            rows = recv_ref[quad, :, at].reshape(CENT_BLK, EMBED_WIDTH)
            cent_ref[((quad // cores) * depth + at) * cores + quad % cores] = rows.T
            return carry

        lax.fori_loop(0, depth, turn, 0, unroll=4)

    def spread(block, side):
        inverse = inv_ref[side]

        def piece(k):
            slot = slots[block * 3 + k]
            left = exp_ref[side, k, :, :128] * inverse
            right = exp_ref[side, k, :, 128:] * inverse
            weights = jnp.concatenate([left, right], axis=1)
            cnt_ref[slot] += jnp.sum(weights.reshape(TOK_BLK // 8, 8, CENT_BLK), axis=0)
            acc_ref[slot] += jnp.dot(
                turned_ref[block], weights.astype(jnp.bfloat16), preferred_element_type=jnp.float32
            )

        return piece

    def score(block, side):
        tok = unit_ref[pl.ds(pl.multiple_of(block * TOK_BLK, TOK_BLK), TOK_BLK), :]
        totals = []

        def piece(k):
            slot = slots[block * 3 + k]
            scores = jnp.dot(tok, cent_ref[slot], preferred_element_type=jnp.float32)
            grown = jnp.exp2(scores * EXP2_SCALE)
            exp_ref[side, k] = grown
            part = grown[:, :128] + grown[:, 128:]
            totals.append(part if not totals else totals.pop() + part)

        def close():
            total = jnp.sum(totals[0], axis=1, keepdims=True)
            inv_ref[side] = jnp.broadcast_to(1.0 / total, inv_ref.shape[1:])

        return piece, close

    def round_of(index, carry):
        for u in range(unroll):
            block = unroll * index + u
            piece_a, close = score(block, u % 2)
            piece_b = spread(jnp.maximum(block - 1, 0), (u + 1) % 2)
            for k in range(3):
                piece_a(k)
                piece_b(k)
            close()
        return carry

    lax.fori_loop(0, blocks // unroll, round_of, 0)
    piece = spread(blocks - 1, 1)
    for k in range(3):
        piece(k)
    finish(ids, out_ref, acc_ref, cnt_ref)


def finish(ids, out_ref, acc_ref, cnt_ref):
    row = lax.broadcasted_iota(jnp.int32, (8, EMBED_WIDTH), 0)

    def write(slot, carry):
        out_ref[slot, :128, :] = acc_ref[slot, :, :128].astype(jnp.bfloat16)
        out_ref[slot, 128:256, :] = acc_ref[slot, :, 128:].astype(jnp.bfloat16)
        counts = jnp.sum(cnt_ref[slot], axis=0, keepdims=True)
        tile = split_counts(counts[:, :128], counts[:, 128:])
        named = jnp.full(tile.shape, ids[slot].astype(jnp.float32))
        out_ref[slot, CENT_BLK:, :] = jnp.where(row == 4, named, tile.astype(jnp.float32)).astype(jnp.bfloat16)
        return carry

    lax.fori_loop(0, cnt_ref.shape[0], write, 0, unroll=4)


def attend(slots, ids, unit, turned, recv, unroll=4):
    owners = ids.shape[0]
    blocks = turned.shape[0]
    unroll = math.gcd(unroll, blocks)
    pairs = blocks * 3 * TOK_BLK * CENT_BLK
    whole = lambda shape: pl.BlockSpec(
        shape, lambda i, s, n: (0,) * len(shape), pipeline_mode=pl.Buffered(1)
    )
    shape = (owners, MSG_ROWS, EMBED_WIDTH)
    return pl.pallas_call(
        functools.partial(attend_kernel, unroll),
        grid_spec=pltpu.PrefetchScalarGridSpec(
            num_scalar_prefetch=2,
            grid=(1,),
            in_specs=[whole(unit.shape), whole(turned.shape), whole(recv.shape)],
            out_specs=whole(shape),
            scratch_shapes=[
                pltpu.VMEM((owners, EMBED_WIDTH, CENT_BLK), jnp.float32),
                pltpu.VMEM((owners, 8, CENT_BLK), jnp.float32),
                pltpu.VMEM((2, 3, TOK_BLK, CENT_BLK), jnp.float32),
                pltpu.VMEM((2, TOK_BLK, 128), jnp.float32),
                pltpu.VMEM((owners, EMBED_WIDTH, CENT_BLK), jnp.bfloat16),
            ],
        ),
        out_shape=jax.ShapeDtypeStruct(shape, jnp.bfloat16),
        compiler_params=pltpu.CompilerParams(
            vmem_limit_bytes=28 << 20
        ),
        cost_estimate=pl.CostEstimate(
            flops=pairs * EMBED_WIDTH * 4, transcendentals=pairs, bytes_accessed=unit.size * 6
        ),
        name="attend",
    )(slots, ids, unit, turned, recv)


def pick_kernel(asked, zpos, *refs):
    pieces, out_ref = refs[:-1], refs[-1]
    depth = out_ref.shape[1]
    half = pieces[0].shape[0]

    def fill(peer, carry):
        for at in range(depth):
            source = zpos[at]
            inner = jnp.maximum(asked[peer * depth + source], 0)
            low = jnp.where(inner < half, inner, inner - half)
            picked = jnp.where(inner < half, pieces[at][low], pieces[depth + at][low])
            out_ref[peer, source] = picked
        return carry

    lax.fori_loop(0, out_ref.shape[0], fill, 0, unroll=2)


def pick(asked, zpos, pieces, peers):
    depth = len(pieces) // 2
    rows = pieces[0].shape[1]
    shape = (peers, depth, rows, EMBED_WIDTH)
    return pl.pallas_call(
        pick_kernel,
        grid_spec=pltpu.PrefetchScalarGridSpec(
            num_scalar_prefetch=2,
            grid=(1,),
            in_specs=[
                pl.BlockSpec(p.shape, lambda i, s, n: (0, 0, 0), pipeline_mode=pl.Buffered(1))
                for p in pieces
            ],
            out_specs=pl.BlockSpec(shape, lambda i, s, n: (0, 0, 0, 0), pipeline_mode=pl.Buffered(1)),
        ),
        out_shape=jax.ShapeDtypeStruct(shape, jnp.bfloat16),
        compiler_params=pltpu.CompilerParams(vmem_limit_bytes=8 << 20),
        cost_estimate=pl.CostEstimate(flops=0, transcendentals=0, bytes_accessed=4 << 20),
        name="pick",
    )(asked, zpos, *pieces)


def gather_ring(low, high, axis):
    depth = lax.axis_size(axis)
    up = [(i, (i + 1) % depth) for i in range(depth)]
    down = [(i, (i - 1) % depth) for i in range(depth)]
    lows, highs = {0: low}, {0: high}
    rise, fall = depth // 2, (depth - 1) // 2
    for step in range(1, rise + 1):
        lows[step] = lax.ppermute(lows[step - 1], axis, up)
        highs[-step] = lax.ppermute(highs[1 - step], axis, down)
        if step <= fall:
            highs[step] = lax.ppermute(highs[step - 1], axis, up)
            lows[-step] = lax.ppermute(lows[1 - step], axis, down)
    lows = {away % depth: piece for away, piece in lows.items()}
    highs = {away % depth: piece for away, piece in highs.items()}
    return [lows[k] for k in range(depth)] + [highs[k] for k in range(depth)]


def collect_kernel(asked, back_ref, out_ref, acc_ref):
    acc_ref[...] = jnp.zeros_like(acc_ref)

    def add(source, carry):
        inner = asked[source]

        @pl.when(inner >= 0)
        def _():
            acc_ref[inner] += back_ref[source].astype(jnp.float32)

        return carry

    lax.fori_loop(0, back_ref.shape[0], add, 0)

    def write(inner, carry):
        out_ref[inner, :CENT_BLK, :] = acc_ref[inner, :CENT_BLK, :].astype(jnp.bfloat16)
        tile = acc_ref[inner, CENT_BLK:, :]
        totals = tile[0:2] + tile[2:4]
        out_ref[inner, CENT_BLK:, :] = split_counts(totals[0:1], totals[1:2])
        return carry

    lax.fori_loop(0, out_ref.shape[0], write, 0)


def collect(asked, back):
    shape = (BPO, MSG_ROWS, EMBED_WIDTH)
    return pl.pallas_call(
        collect_kernel,
        grid_spec=pltpu.PrefetchScalarGridSpec(
            num_scalar_prefetch=1,
            grid=(1,),
            in_specs=[pl.BlockSpec(back.shape, lambda i, s: (0, 0, 0), pipeline_mode=pl.Buffered(1))],
            out_specs=pl.BlockSpec(shape, lambda i, s: (0, 0, 0), pipeline_mode=pl.Buffered(1)),
            scratch_shapes=[pltpu.VMEM(shape, jnp.float32)],
        ),
        out_shape=jax.ShapeDtypeStruct(shape, jnp.bfloat16),
        compiler_params=pltpu.CompilerParams(vmem_limit_bytes=24 << 20),
        cost_estimate=pl.CostEstimate(
            flops=back.size, transcendentals=0, bytes_accessed=back.size * 4
        ),
        name="collect",
    )(asked, back)


OWNER = ("xlo", "z", "core")
PLANE = ("xlo", "core", "slab")


def shards(tokens, listed, centroids):
    slab_count = lax.axis_size("slab")
    slab_index = lax.axis_index("slab")
    depth = lax.axis_size("z")
    cores = lax.axis_size("core")
    quads = lax.axis_size("xlo") * cores
    owner_count = quads * depth
    peers = quads * slab_count
    share_blocks = BPO // slab_count
    share_rows = CENT_BLK // slab_count

    blocks = centroids.reshape(BPO, CENT_BLK, EMBED_WIDTH)
    piece = lax.dynamic_slice_in_dim(blocks, slab_index * share_rows, share_rows, 1)
    piece = unit_rows(piece).astype(jnp.bfloat16)
    pieces = gather_ring(piece[:BPO // 2], piece[BPO // 2:], "z")

    owner_ids = jnp.arange(owner_count, dtype=jnp.int32)
    group_of = listed // BPO
    inner_ids = listed % BPO
    matches = group_of[:, :, None] == owner_ids
    wanted = jnp.max(jnp.where(matches, inner_ids[:, :, None] + 1, 0), axis=(0, 1)) - 1
    by_quad = wanted.reshape(-1, depth, cores).transpose(0, 2, 1).reshape(quads, 1, depth)
    requests = jnp.broadcast_to(by_quad, (quads, slab_count, depth)).reshape(peers, 1, depth)
    asked = lax.all_to_all(requests, PLANE, split_axis=0, concat_axis=0, tiled=True).reshape(-1)

    zpos = (lax.axis_index("z") - jnp.arange(depth, dtype=jnp.int32)) % depth
    picked = pick(asked, zpos, pieces, peers)
    recv = lax.all_to_all(picked, PLANE, split_axis=0, concat_axis=0, tiled=True)
    recv = recv.reshape(quads, slab_count, depth, share_rows, EMBED_WIDTH)

    tokens, _ = lax.optimization_barrier((tokens, picked))
    unit, turned = prepare(tokens)
    partial = attend(group_of.reshape(-1), wanted, unit, turned, recv)
    back = lax.all_to_all(partial, OWNER, split_axis=0, concat_axis=0, tiled=True)
    own = collect(back[:, CENT_BLK + 4, 0].astype(jnp.int32), back)
    slabs = lax.all_to_all(own, "slab", split_axis=0, concat_axis=0, tiled=True)
    slabs = slabs.reshape(slab_count, share_blocks, MSG_ROWS, EMBED_WIDTH)

    totals = jnp.sum(slabs.astype(jnp.float32), axis=0)
    counts = (totals[:, CENT_BLK:CENT_BLK + 2] + totals[:, CENT_BLK + 2:CENT_BLK + 4]).reshape(-1)
    halves = totals[:, :CENT_BLK].reshape(share_blocks, 2, EMBED_WIDTH, CENT_BLK // 2)
    sums = halves.transpose(0, 1, 3, 2).reshape(-1, EMBED_WIDTH)
    rows = share_blocks * CENT_BLK
    mine = unit_rows(lax.dynamic_slice_in_dim(centroids, slab_index * rows, rows, 0))
    refined = (sums + PRIOR_WEIGHT * mine) / (counts[:, None] + PRIOR_WEIGHT)
    return refined, counts


def solution(mesh):
    owners, slabs = mesh.devices.shape
    split = Mesh(mesh.devices.reshape(2, owners // 4, 2, slabs), OWNER + ("slab",))
    every = OWNER + ("slab",)
    placed = (P(every, None), P(every, None), P(OWNER, None))
    return jax.shard_map(
        shards,
        mesh=split,
        in_specs=placed,
        out_specs=(P(every, None), P(every)),
        check_vma=False,
    )
```

```python
import functools
import math

import jax
import jax.numpy as jnp
from jax import lax
from jax.experimental import pallas as pl
from jax.experimental.pallas import tpu as pltpu
from jax.sharding import Mesh
from jax.sharding import PartitionSpec as P

EMBED_WIDTH = 128
CENT_BLK = 256
TOK_BLK = 256
BPO = 32
MSG_ROWS = CENT_BLK + 8

SOFTMAX_TEMP = 0.1
PRIOR_WEIGHT = 4.0
EPSILON = 1e-06
EXP2_SCALE = math.log2(math.e) / (EMBED_WIDTH * SOFTMAX_TEMP)


def unit_rows(values):
    widened = values.astype(jnp.float32)
    return widened * lax.rsqrt(jnp.mean(widened * widened, axis=-1, keepdims=True) + EPSILON)


def split_counts(totals_a, totals_b):
    row = lax.broadcasted_iota(jnp.int32, (8, EMBED_WIDTH), 0)
    heads = jnp.where(row % 2 == 0, totals_a, totals_b)
    rounded = heads.astype(jnp.bfloat16).astype(jnp.float32)
    tails = heads - rounded
    tile = jnp.where(row < 2, rounded, jnp.where(row < 4, tails, 0.0))
    return tile.astype(jnp.bfloat16)


def prepare_kernel(tok_ref, unit_ref, turned_ref):
    tok = unit_rows(tok_ref[...]).astype(jnp.bfloat16)
    unit_ref[...] = tok
    for at in range(turned_ref.shape[0]):
        turned_ref[at] = tok[at * TOK_BLK:(at + 1) * TOK_BLK].T


def prepare(tokens, per_step=4):
    blocks = tokens.shape[0] // TOK_BLK
    per_step = math.gcd(per_step, blocks)
    rows = per_step * TOK_BLK
    return pl.pallas_call(
        prepare_kernel,
        grid=(blocks // per_step,),
        in_specs=[pl.BlockSpec((rows, EMBED_WIDTH), lambda i: (i, 0))],
        out_specs=(
            pl.BlockSpec((rows, EMBED_WIDTH), lambda i: (i, 0)),
            pl.BlockSpec((per_step, EMBED_WIDTH, TOK_BLK), lambda i: (i, 0, 0)),
        ),
        out_shape=(
            jax.ShapeDtypeStruct(tokens.shape, jnp.bfloat16),
            jax.ShapeDtypeStruct((blocks, EMBED_WIDTH, TOK_BLK), jnp.bfloat16),
        ),
        compiler_params=pltpu.CompilerParams(vmem_limit_bytes=56 << 20),
        cost_estimate=pl.CostEstimate(
            flops=tokens.size * 4, transcendentals=tokens.shape[0], bytes_accessed=tokens.size * 6
        ),
        name="prepare",
    )(tokens)


def attend_kernel(
    unroll, parts, slots, ids, unit_hbm, turned_hbm, recv_ref, out_ref,
    acc_ref, cnt_ref, exp_ref, inv_ref, cent_ref, unit_ref, turned_ref, unit_sems, turned_sems,
):
    blocks = turned_ref.shape[0]
    share = blocks // parts

    def unit_copy(part):
        rows = pl.ds(pl.multiple_of(part * share * TOK_BLK, TOK_BLK), share * TOK_BLK)
        return pltpu.make_async_copy(unit_hbm.at[rows], unit_ref.at[rows], unit_sems.at[part])

    def turned_copy(part):
        rows = pl.ds(part * share, share)
        return pltpu.make_async_copy(turned_hbm.at[rows], turned_ref.at[rows], turned_sems.at[part])

    for part in range(parts):
        unit_copy(part).start()
        turned_copy(part).start()
    acc_ref[...] = jnp.zeros_like(acc_ref)
    cnt_ref[...] = jnp.zeros_like(cnt_ref)
    exp_ref[1] = jnp.zeros(exp_ref.shape[1:], exp_ref.dtype)
    inv_ref[1] = jnp.zeros(inv_ref.shape[1:], inv_ref.dtype)
    quads, _, depth = recv_ref.shape[:3]
    cores = 2
    for quad in range(quads):
        def turn(at, carry):
            rows = recv_ref[quad, :, at].reshape(CENT_BLK, EMBED_WIDTH)
            cent_ref[((quad // cores) * depth + at) * cores + quad % cores] = rows.T
            return carry

        lax.fori_loop(0, depth, turn, 0, unroll=4)

    def spread(block, side):
        inverse = inv_ref[side]

        def piece(k):
            slot = slots[block * 3 + k]
            left = exp_ref[side, k, :, :128] * inverse
            right = exp_ref[side, k, :, 128:] * inverse
            weights = jnp.concatenate([left, right], axis=1)
            cnt_ref[slot] += jnp.sum(weights.reshape(TOK_BLK // 8, 8, CENT_BLK), axis=0)
            acc_ref[slot] += jnp.dot(
                turned_ref[block], weights.astype(jnp.bfloat16), preferred_element_type=jnp.float32
            )

        return piece

    def score(block, side):
        tok = unit_ref[pl.ds(pl.multiple_of(block * TOK_BLK, TOK_BLK), TOK_BLK), :]
        totals = []

        def piece(k):
            slot = slots[block * 3 + k]
            scores = jnp.dot(tok, cent_ref[slot], preferred_element_type=jnp.float32)
            grown = jnp.exp2(scores * EXP2_SCALE)
            exp_ref[side, k] = grown
            part = grown[:, :128] + grown[:, 128:]
            totals.append(part if not totals else totals.pop() + part)

        def close():
            total = jnp.sum(totals[0], axis=1, keepdims=True)
            inv_ref[side] = jnp.broadcast_to(1.0 / total, inv_ref.shape[1:])

        return piece, close

    def round_of(index, carry):
        @pl.when(index % (share // unroll) == 0)
        def _():
            unit_copy(index // (share // unroll)).wait()
            turned_copy(index // (share // unroll)).wait()

        for u in range(unroll):
            block = unroll * index + u
            piece_a, close = score(block, u % 2)
            piece_b = spread(jnp.maximum(block - 1, 0), (u + 1) % 2)
            for k in range(3):
                piece_a(k)
                piece_b(k)
            close()
        return carry

    lax.fori_loop(0, blocks // unroll, round_of, 0)
    piece = spread(blocks - 1, 1)
    for k in range(3):
        piece(k)
    finish(ids, out_ref, acc_ref, cnt_ref)


def finish(ids, out_ref, acc_ref, cnt_ref):
    row = lax.broadcasted_iota(jnp.int32, (8, EMBED_WIDTH), 0)

    def write(slot, carry):
        out_ref[slot, :128, :] = acc_ref[slot, :, :128].astype(jnp.bfloat16)
        out_ref[slot, 128:256, :] = acc_ref[slot, :, 128:].astype(jnp.bfloat16)
        counts = jnp.sum(cnt_ref[slot], axis=0, keepdims=True)
        tile = split_counts(counts[:, :128], counts[:, 128:])
        named = jnp.full(tile.shape, ids[slot].astype(jnp.float32))
        out_ref[slot, CENT_BLK:, :] = jnp.where(row == 4, named, tile.astype(jnp.float32)).astype(jnp.bfloat16)
        return carry

    lax.fori_loop(0, cnt_ref.shape[0], write, 0, unroll=4)


def attend(slots, ids, unit, turned, recv, unroll=4):
    owners = ids.shape[0]
    blocks = turned.shape[0]
    unroll = math.gcd(unroll, blocks)
    parts = math.gcd(4, blocks // unroll)
    pairs = blocks * 3 * TOK_BLK * CENT_BLK
    whole = lambda shape: pl.BlockSpec(
        shape, lambda i, s, n: (0,) * len(shape), pipeline_mode=pl.Buffered(1)
    )
    shape = (owners, MSG_ROWS, EMBED_WIDTH)
    return pl.pallas_call(
        functools.partial(attend_kernel, unroll, parts),
        grid_spec=pltpu.PrefetchScalarGridSpec(
            num_scalar_prefetch=2,
            grid=(1,),
            in_specs=[
                pl.BlockSpec(memory_space=pl.ANY),
                pl.BlockSpec(memory_space=pl.ANY),
                whole(recv.shape),
            ],
            out_specs=whole(shape),
            scratch_shapes=[
                pltpu.VMEM((owners, EMBED_WIDTH, CENT_BLK), jnp.float32),
                pltpu.VMEM((owners, 8, CENT_BLK), jnp.float32),
                pltpu.VMEM((2, 3, TOK_BLK, CENT_BLK), jnp.float32),
                pltpu.VMEM((2, TOK_BLK, 128), jnp.float32),
                pltpu.VMEM((owners, EMBED_WIDTH, CENT_BLK), jnp.bfloat16),
                pltpu.VMEM(unit.shape, jnp.bfloat16),
                pltpu.VMEM(turned.shape, jnp.bfloat16),
                pltpu.SemaphoreType.DMA((parts,)),
                pltpu.SemaphoreType.DMA((parts,)),
            ],
        ),
        out_shape=jax.ShapeDtypeStruct(shape, jnp.bfloat16),
        compiler_params=pltpu.CompilerParams(vmem_limit_bytes=48 << 20),
        cost_estimate=pl.CostEstimate(
            flops=pairs * EMBED_WIDTH * 4, transcendentals=pairs, bytes_accessed=unit.size * 6
        ),
        name="attend",
    )(slots, ids, unit, turned, recv)


def pick_kernel(asked, zpos, *refs):
    pieces, out_ref = refs[:-1], refs[-1]
    depth = out_ref.shape[1]
    half = pieces[0].shape[0]

    def fill(peer, carry):
        for at in range(depth):
            source = zpos[at]
            inner = jnp.maximum(asked[peer * depth + source], 0)
            low = jnp.where(inner < half, inner, inner - half)
            picked = jnp.where(inner < half, pieces[at][low], pieces[depth + at][low])
            out_ref[peer, source] = picked
        return carry

    lax.fori_loop(0, out_ref.shape[0], fill, 0, unroll=2)


def pick(asked, zpos, pieces, peers):
    depth = len(pieces) // 2
    rows = pieces[0].shape[1]
    shape = (peers, depth, rows, EMBED_WIDTH)
    return pl.pallas_call(
        pick_kernel,
        grid_spec=pltpu.PrefetchScalarGridSpec(
            num_scalar_prefetch=2,
            grid=(1,),
            in_specs=[
                pl.BlockSpec(p.shape, lambda i, s, n: (0, 0, 0), pipeline_mode=pl.Buffered(1))
                for p in pieces
            ],
            out_specs=pl.BlockSpec(shape, lambda i, s, n: (0, 0, 0, 0), pipeline_mode=pl.Buffered(1)),
        ),
        out_shape=jax.ShapeDtypeStruct(shape, jnp.bfloat16),
        compiler_params=pltpu.CompilerParams(vmem_limit_bytes=8 << 20),
        cost_estimate=pl.CostEstimate(flops=0, transcendentals=0, bytes_accessed=4 << 20),
        name="pick",
    )(asked, zpos, *pieces)


def gather_ring(low, high, axis):
    depth = lax.axis_size(axis)
    up = [(i, (i + 1) % depth) for i in range(depth)]
    down = [(i, (i - 1) % depth) for i in range(depth)]
    lows, highs = {0: low}, {0: high}
    rise, fall = depth // 2, (depth - 1) // 2
    for step in range(1, rise + 1):
        lows[step] = lax.ppermute(lows[step - 1], axis, up)
        highs[-step] = lax.ppermute(highs[1 - step], axis, down)
        if step <= fall:
            highs[step] = lax.ppermute(highs[step - 1], axis, up)
            lows[-step] = lax.ppermute(lows[1 - step], axis, down)
    lows = {away % depth: piece for away, piece in lows.items()}
    highs = {away % depth: piece for away, piece in highs.items()}
    return [lows[k] for k in range(depth)] + [highs[k] for k in range(depth)]


def collect_kernel(asked, back_ref, out_ref, acc_ref):
    acc_ref[...] = jnp.zeros_like(acc_ref)

    def add(source, carry):
        inner = asked[source]

        @pl.when(inner >= 0)
        def _():
            acc_ref[inner] += back_ref[source].astype(jnp.float32)

        return carry

    lax.fori_loop(0, back_ref.shape[0], add, 0)

    def write(inner, carry):
        out_ref[inner, :CENT_BLK, :] = acc_ref[inner, :CENT_BLK, :].astype(jnp.bfloat16)
        tile = acc_ref[inner, CENT_BLK:, :]
        totals = tile[0:2] + tile[2:4]
        out_ref[inner, CENT_BLK:, :] = split_counts(totals[0:1], totals[1:2])
        return carry

    lax.fori_loop(0, out_ref.shape[0], write, 0)


def collect(asked, back):
    shape = (BPO, MSG_ROWS, EMBED_WIDTH)
    return pl.pallas_call(
        collect_kernel,
        grid_spec=pltpu.PrefetchScalarGridSpec(
            num_scalar_prefetch=1,
            grid=(1,),
            in_specs=[pl.BlockSpec(back.shape, lambda i, s: (0, 0, 0), pipeline_mode=pl.Buffered(1))],
            out_specs=pl.BlockSpec(shape, lambda i, s: (0, 0, 0), pipeline_mode=pl.Buffered(1)),
            scratch_shapes=[pltpu.VMEM(shape, jnp.float32)],
        ),
        out_shape=jax.ShapeDtypeStruct(shape, jnp.bfloat16),
        compiler_params=pltpu.CompilerParams(vmem_limit_bytes=24 << 20),
        cost_estimate=pl.CostEstimate(
            flops=back.size, transcendentals=0, bytes_accessed=back.size * 4
        ),
        name="collect",
    )(asked, back)


OWNER = ("xlo", "z", "core")
PLANE = ("xlo", "core", "slab")


def shards(tokens, listed, centroids):
    slab_count = lax.axis_size("slab")
    slab_index = lax.axis_index("slab")
    depth = lax.axis_size("z")
    cores = lax.axis_size("core")
    quads = lax.axis_size("xlo") * cores
    owner_count = quads * depth
    peers = quads * slab_count
    share_blocks = BPO // slab_count
    share_rows = CENT_BLK // slab_count

    blocks = centroids.reshape(BPO, CENT_BLK, EMBED_WIDTH)
    piece = lax.dynamic_slice_in_dim(blocks, slab_index * share_rows, share_rows, 1)
    piece = unit_rows(piece).astype(jnp.bfloat16)
    pieces = gather_ring(piece[:BPO // 2], piece[BPO // 2:], "z")

    owner_ids = jnp.arange(owner_count, dtype=jnp.int32)
    group_of = listed // BPO
    inner_ids = listed % BPO
    matches = group_of[:, :, None] == owner_ids
    wanted = jnp.max(jnp.where(matches, inner_ids[:, :, None] + 1, 0), axis=(0, 1)) - 1
    by_quad = wanted.reshape(-1, depth, cores).transpose(0, 2, 1).reshape(quads, 1, depth)
    requests = jnp.broadcast_to(by_quad, (quads, slab_count, depth)).reshape(peers, 1, depth)
    asked = lax.all_to_all(requests, PLANE, split_axis=0, concat_axis=0, tiled=True)
    asked = asked.reshape(-1)

    zpos = (lax.axis_index("z") - jnp.arange(depth, dtype=jnp.int32)) % depth
    picked = pick(asked, zpos, pieces, peers)
    recv = lax.all_to_all(picked, PLANE, split_axis=0, concat_axis=0, tiled=True)
    recv = recv.reshape(quads, slab_count, depth, share_rows, EMBED_WIDTH)

    tokens, _ = lax.optimization_barrier((tokens, picked))
    unit, turned = prepare(tokens)
    partial = attend(group_of.reshape(-1), wanted, unit, turned, recv)
    back = lax.all_to_all(partial, OWNER, split_axis=0, concat_axis=0, tiled=True)
    own = collect(back[:, CENT_BLK + 4, 0].astype(jnp.int32), back)
    slabs = lax.all_to_all(own, "slab", split_axis=0, concat_axis=0, tiled=True)
    slabs = slabs.reshape(slab_count, share_blocks, MSG_ROWS, EMBED_WIDTH)

    totals = jnp.sum(slabs.astype(jnp.float32), axis=0)
    counts = (totals[:, CENT_BLK:CENT_BLK + 2] + totals[:, CENT_BLK + 2:CENT_BLK + 4]).reshape(-1)
    halves = totals[:, :CENT_BLK].reshape(share_blocks, 2, EMBED_WIDTH, CENT_BLK // 2)
    sums = halves.transpose(0, 1, 3, 2).reshape(-1, EMBED_WIDTH)
    rows = share_blocks * CENT_BLK
    mine = unit_rows(lax.dynamic_slice_in_dim(centroids, slab_index * rows, rows, 0))
    refined = (sums + PRIOR_WEIGHT * mine) / (counts[:, None] + PRIOR_WEIGHT)
    return refined, counts


def solution(mesh):
    owners, slabs = mesh.devices.shape
    split = Mesh(mesh.devices.reshape(2, owners // 4, 2, slabs), OWNER + ("slab",))
    every = OWNER + ("slab",)
    placed = (P(every, None), P(every, None), P(OWNER, None))
    return jax.shard_map(
        lambda *args: shards(*args),
        mesh=split,
        in_specs=placed,
        out_specs=(P(every, None), P(every)),
        check_vma=False,
    )
```

```python
import functools
import math

import jax
import jax.numpy as jnp
from jax import lax
from jax.experimental import pallas as pl
from jax.experimental.pallas import tpu as pltpu
from jax.sharding import Mesh
from jax.sharding import PartitionSpec as P

EMBED_WIDTH = 128
CENT_BLK = 256
TOK_BLK = 256
BPO = 32
MSG_ROWS = CENT_BLK + 8

SOFTMAX_TEMP = 0.1
PRIOR_WEIGHT = 4.0
EPSILON = 1e-06
EXP2_SCALE = math.log2(math.e) / (EMBED_WIDTH * SOFTMAX_TEMP)


def unit_rows(values):
    widened = values.astype(jnp.float32)
    return widened * lax.rsqrt(jnp.mean(widened * widened, axis=-1, keepdims=True) + EPSILON)


def split_counts(totals_a, totals_b):
    row = lax.broadcasted_iota(jnp.int32, (8, EMBED_WIDTH), 0)
    heads = jnp.where(row % 2 == 0, totals_a, totals_b)
    rounded = heads.astype(jnp.bfloat16).astype(jnp.float32)
    tails = heads - rounded
    tile = jnp.where(row < 2, rounded, jnp.where(row < 4, tails, 0.0))
    return tile.astype(jnp.bfloat16)


def prepare_kernel(tok_ref, unit_ref, turned_ref):
    tok = unit_rows(tok_ref[...]).astype(jnp.bfloat16)
    unit_ref[...] = tok
    for at in range(turned_ref.shape[0]):
        turned_ref[at] = tok[at * TOK_BLK:(at + 1) * TOK_BLK].T


def prepare(tokens, per_step=16):
    blocks = tokens.shape[0] // TOK_BLK
    per_step = math.gcd(per_step, blocks)
    rows = per_step * TOK_BLK
    return pl.pallas_call(
        prepare_kernel,
        grid=(blocks // per_step,),
        in_specs=[pl.BlockSpec((rows, EMBED_WIDTH), lambda i: (i, 0))],
        out_specs=(
            pl.BlockSpec((rows, EMBED_WIDTH), lambda i: (i, 0)),
            pl.BlockSpec((per_step, EMBED_WIDTH, TOK_BLK), lambda i: (i, 0, 0)),
        ),
        out_shape=(
            jax.ShapeDtypeStruct(tokens.shape, jnp.bfloat16),
            jax.ShapeDtypeStruct((blocks, EMBED_WIDTH, TOK_BLK), jnp.bfloat16),
        ),
        compiler_params=pltpu.CompilerParams(vmem_limit_bytes=56 << 20),
        cost_estimate=pl.CostEstimate(
            flops=tokens.size * 4, transcendentals=tokens.shape[0], bytes_accessed=tokens.size * 6
        ),
        name="prepare",
    )(tokens)


def attend_kernel(
    unroll, parts, slots, ids, zpos, unit_hbm, turned_hbm, near_ref, far_ref, out_ref,
    acc_ref, cnt_ref, exp_ref, inv_ref, cent_ref, unit_ref, turned_ref, unit_sems, turned_sems,
):
    blocks = turned_ref.shape[0]
    share = blocks // parts

    def unit_copy(part):
        rows = pl.ds(pl.multiple_of(part * share * TOK_BLK, TOK_BLK), share * TOK_BLK)
        return pltpu.make_async_copy(unit_hbm.at[rows], unit_ref.at[rows], unit_sems.at[part])

    def turned_copy(part):
        rows = pl.ds(part * share, share)
        return pltpu.make_async_copy(turned_hbm.at[rows], turned_ref.at[rows], turned_sems.at[part])

    for part in range(parts):
        unit_copy(part).start()
        turned_copy(part).start()
    acc_ref[...] = jnp.zeros_like(acc_ref)
    cnt_ref[...] = jnp.zeros_like(cnt_ref)
    exp_ref[1] = jnp.zeros(exp_ref.shape[1:], exp_ref.dtype)
    inv_ref[1] = jnp.zeros(inv_ref.shape[1:], inv_ref.dtype)
    depth = near_ref.shape[2] + far_ref.shape[2]
    cores = 2
    for first, recv_ref in ((0, near_ref), (near_ref.shape[2], far_ref)):
        def turn(quad, carry):
            for at in range(recv_ref.shape[2]):
                rows = recv_ref[quad, :, at].reshape(CENT_BLK, EMBED_WIDTH)
                slot = ((quad // cores) * depth + zpos[first + at]) * cores + quad % cores
                cent_ref[slot] = rows.T
            return carry

        lax.fori_loop(0, near_ref.shape[0], turn, 0)

    def spread(block, side):
        inverse = inv_ref[side]

        def piece(k):
            slot = slots[block * 3 + k]
            left = exp_ref[side, k, :, :128] * inverse
            right = exp_ref[side, k, :, 128:] * inverse
            weights = jnp.concatenate([left, right], axis=1)
            cnt_ref[slot] += jnp.sum(weights.reshape(TOK_BLK // 8, 8, CENT_BLK), axis=0)
            acc_ref[slot] += jnp.dot(
                turned_ref[block], weights.astype(jnp.bfloat16), preferred_element_type=jnp.float32
            )

        return piece

    def score(block, side):
        tok = unit_ref[pl.ds(pl.multiple_of(block * TOK_BLK, TOK_BLK), TOK_BLK), :]
        totals = []

        def piece(k):
            slot = slots[block * 3 + k]
            scores = jnp.dot(tok, cent_ref[slot], preferred_element_type=jnp.float32)
            grown = jnp.exp2(scores * EXP2_SCALE)
            exp_ref[side, k] = grown
            part = grown[:, :128] + grown[:, 128:]
            totals.append(part if not totals else totals.pop() + part)

        def close():
            total = jnp.sum(totals[0], axis=1, keepdims=True)
            inv_ref[side] = jnp.broadcast_to(1.0 / total, inv_ref.shape[1:])

        return piece, close

    def round_of(index, carry):
        @pl.when(index % (share // unroll) == 0)
        def _():
            unit_copy(index // (share // unroll)).wait()
            turned_copy(index // (share // unroll)).wait()

        for u in range(unroll):
            block = unroll * index + u
            piece_a, close = score(block, u % 2)
            piece_b = spread(jnp.maximum(block - 1, 0), (u + 1) % 2)
            for k in range(3):
                piece_a(k)
                piece_b(k)
            close()
        return carry

    lax.fori_loop(0, blocks // unroll, round_of, 0)
    piece = spread(blocks - 1, 1)
    for k in range(3):
        piece(k)
    finish(ids, out_ref, acc_ref, cnt_ref)


def finish(ids, out_ref, acc_ref, cnt_ref):
    row = lax.broadcasted_iota(jnp.int32, (8, EMBED_WIDTH), 0)

    def write(slot, carry):
        out_ref[slot, :128, :] = acc_ref[slot, :, :128].astype(jnp.bfloat16)
        out_ref[slot, 128:256, :] = acc_ref[slot, :, 128:].astype(jnp.bfloat16)
        counts = jnp.sum(cnt_ref[slot], axis=0, keepdims=True)
        tile = split_counts(counts[:, :128], counts[:, 128:])
        named = jnp.full(tile.shape, ids[slot].astype(jnp.float32))
        out_ref[slot, CENT_BLK:, :] = jnp.where(row == 4, named, tile.astype(jnp.float32)).astype(jnp.bfloat16)
        return carry

    lax.fori_loop(0, cnt_ref.shape[0], write, 0, unroll=4)


def attend(slots, ids, zpos, unit, turned, near, far, unroll=4):
    owners = ids.shape[0]
    blocks = turned.shape[0]
    unroll = math.gcd(unroll, blocks)
    parts = math.gcd(4, blocks // unroll)
    pairs = blocks * 3 * TOK_BLK * CENT_BLK
    whole = lambda shape: pl.BlockSpec(
        shape, lambda i, s, n, z: (0,) * len(shape), pipeline_mode=pl.Buffered(1)
    )
    shape = (owners, MSG_ROWS, EMBED_WIDTH)
    return pl.pallas_call(
        functools.partial(attend_kernel, unroll, parts),
        grid_spec=pltpu.PrefetchScalarGridSpec(
            num_scalar_prefetch=3,
            grid=(1,),
            in_specs=[
                pl.BlockSpec(memory_space=pl.ANY),
                pl.BlockSpec(memory_space=pl.ANY),
                whole(near.shape),
                whole(far.shape),
            ],
            out_specs=whole(shape),
            scratch_shapes=[
                pltpu.VMEM((owners, EMBED_WIDTH, CENT_BLK), jnp.float32),
                pltpu.VMEM((owners, 8, CENT_BLK), jnp.float32),
                pltpu.VMEM((2, 3, TOK_BLK, CENT_BLK), jnp.float32),
                pltpu.VMEM((2, TOK_BLK, 128), jnp.float32),
                pltpu.VMEM((owners, EMBED_WIDTH, CENT_BLK), jnp.bfloat16),
                pltpu.VMEM(unit.shape, jnp.bfloat16),
                pltpu.VMEM(turned.shape, jnp.bfloat16),
                pltpu.SemaphoreType.DMA((parts,)),
                pltpu.SemaphoreType.DMA((parts,)),
            ],
        ),
        out_shape=jax.ShapeDtypeStruct(shape, jnp.bfloat16),
        compiler_params=pltpu.CompilerParams(vmem_limit_bytes=48 << 20),
        cost_estimate=pl.CostEstimate(
            flops=pairs * EMBED_WIDTH * 4, transcendentals=pairs, bytes_accessed=unit.size * 6
        ),
        name="attend",
    )(slots, ids, zpos, unit, turned, near, far)


def pick_kernel(asked, zpos, depth, *refs):
    pieces, out_ref = refs[:-1], refs[-1]

    def fill(peer, carry):
        for at in range(len(pieces)):
            inner = asked[peer * depth[0] + zpos[at]]
            out_ref[peer, at] = pieces[at][jnp.maximum(inner, 0)]
        return carry

    lax.fori_loop(0, out_ref.shape[0], fill, 0, unroll=4)


def pick(asked, zpos, pieces, peers):
    rows = pieces[0].shape[1]
    shape = (peers, len(pieces), rows, EMBED_WIDTH)
    depth = jnp.full((1,), asked.shape[0] // peers, jnp.int32)
    return pl.pallas_call(
        pick_kernel,
        grid_spec=pltpu.PrefetchScalarGridSpec(
            num_scalar_prefetch=3,
            grid=(1,),
            in_specs=[
                pl.BlockSpec(p.shape, lambda i, s, n, d: (0, 0, 0), pipeline_mode=pl.Buffered(1))
                for p in pieces
            ],
            out_specs=pl.BlockSpec(
                shape, lambda i, s, n, d: (0, 0, 0, 0), pipeline_mode=pl.Buffered(1)
            ),
        ),
        out_shape=jax.ShapeDtypeStruct(shape, jnp.bfloat16),
        compiler_params=pltpu.CompilerParams(vmem_limit_bytes=8 << 20),
        cost_estimate=pl.CostEstimate(flops=0, transcendentals=0, bytes_accessed=4 << 20),
        name="pick",
    )(asked, zpos, depth, *pieces)


def gather_ring(piece, axis):
    depth = lax.axis_size(axis)
    up = [(i, (i + 1) % depth) for i in range(depth)]
    down = [(i, (i - 1) % depth) for i in range(depth)]
    pieces = {0: piece}
    rise, fall = depth // 2, (depth - 1) // 2
    for step in range(1, rise + 1):
        pieces[step] = lax.ppermute(pieces[step - 1], axis, up)
        if step <= fall:
            pieces[-step] = lax.ppermute(pieces[1 - step], axis, down)
    pieces = {away % depth: piece for away, piece in pieces.items()}
    return [pieces[k] for k in range(depth)]


def collect_kernel(asked, back_ref, out_ref, acc_ref):
    acc_ref[...] = jnp.zeros_like(acc_ref)

    def add(source, carry):
        inner = asked[source]

        @pl.when(inner >= 0)
        def _():
            acc_ref[inner] += back_ref[source].astype(jnp.float32)

        return carry

    lax.fori_loop(0, back_ref.shape[0], add, 0)

    def write(inner, carry):
        out_ref[inner, :CENT_BLK, :] = acc_ref[inner, :CENT_BLK, :].astype(jnp.bfloat16)
        tile = acc_ref[inner, CENT_BLK:, :]
        totals = tile[0:2] + tile[2:4]
        out_ref[inner, CENT_BLK:, :] = split_counts(totals[0:1], totals[1:2])
        return carry

    lax.fori_loop(0, out_ref.shape[0], write, 0)


def collect(asked, back):
    shape = (BPO, MSG_ROWS, EMBED_WIDTH)
    return pl.pallas_call(
        collect_kernel,
        grid_spec=pltpu.PrefetchScalarGridSpec(
            num_scalar_prefetch=1,
            grid=(1,),
            in_specs=[pl.BlockSpec(back.shape, lambda i, s: (0, 0, 0), pipeline_mode=pl.Buffered(1))],
            out_specs=pl.BlockSpec(shape, lambda i, s: (0, 0, 0), pipeline_mode=pl.Buffered(1)),
            scratch_shapes=[pltpu.VMEM(shape, jnp.float32)],
        ),
        out_shape=jax.ShapeDtypeStruct(shape, jnp.bfloat16),
        compiler_params=pltpu.CompilerParams(vmem_limit_bytes=24 << 20),
        cost_estimate=pl.CostEstimate(
            flops=back.size, transcendentals=0, bytes_accessed=back.size * 4
        ),
        name="collect",
    )(asked, back)


OWNER = ("xlo", "z", "core")
PLANE = ("xlo", "core", "slab")


def shards(tokens, listed, centroids):
    slab_count = lax.axis_size("slab")
    slab_index = lax.axis_index("slab")
    depth = lax.axis_size("z")
    cores = lax.axis_size("core")
    quads = lax.axis_size("xlo") * cores
    owner_count = quads * depth
    peers = quads * slab_count
    share_blocks = BPO // slab_count
    share_rows = CENT_BLK // slab_count

    blocks = centroids.reshape(BPO, CENT_BLK, EMBED_WIDTH)
    piece = lax.dynamic_slice_in_dim(blocks, slab_index * share_rows, share_rows, 1)
    piece = unit_rows(piece).astype(jnp.bfloat16)
    pieces = gather_ring(piece, "z")

    owner_ids = jnp.arange(owner_count, dtype=jnp.int32)
    group_of = listed // BPO
    inner_ids = listed % BPO
    matches = group_of[:, :, None] == owner_ids
    wanted = jnp.max(jnp.where(matches, inner_ids[:, :, None] + 1, 0), axis=(0, 1)) - 1
    by_quad = wanted.reshape(-1, depth, cores).transpose(0, 2, 1).reshape(quads, 1, depth)
    requests = jnp.broadcast_to(by_quad, (quads, slab_count, depth)).reshape(peers, 1, depth)
    asked = lax.all_to_all(requests, PLANE, split_axis=0, concat_axis=0, tiled=True)
    asked = asked.reshape(-1)

    reach = depth // 4
    order = sorted(range(depth), key=lambda away: (min(away, depth - away), away))
    zpos = (lax.axis_index("z") - jnp.array(order, jnp.int32)) % depth
    split = 2 * reach + 1
    received = []
    for part in (slice(0, split), slice(split, depth)):
        picked = pick(asked, zpos[part], [pieces[away] for away in order[part]], peers)
        recv = lax.all_to_all(picked, PLANE, split_axis=0, concat_axis=0, tiled=True)
        received.append(recv.reshape(quads, slab_count, -1, share_rows, EMBED_WIDTH))

    tokens, _ = lax.optimization_barrier((tokens, picked))
    unit, turned = prepare(tokens)
    partial = attend(group_of.reshape(-1), wanted, zpos, unit, turned, *received)
    back = lax.all_to_all(partial, OWNER, split_axis=0, concat_axis=0, tiled=True)
    own = collect(back[:, CENT_BLK + 4, 0].astype(jnp.int32), back)
    slabs = lax.all_to_all(own, "slab", split_axis=0, concat_axis=0, tiled=True)
    slabs = slabs.reshape(slab_count, share_blocks, MSG_ROWS, EMBED_WIDTH)

    totals = jnp.sum(slabs.astype(jnp.float32), axis=0)
    counts = (totals[:, CENT_BLK:CENT_BLK + 2] + totals[:, CENT_BLK + 2:CENT_BLK + 4]).reshape(-1)
    halves = totals[:, :CENT_BLK].reshape(share_blocks, 2, EMBED_WIDTH, CENT_BLK // 2)
    sums = halves.transpose(0, 1, 3, 2).reshape(-1, EMBED_WIDTH)
    rows = share_blocks * CENT_BLK
    mine = unit_rows(lax.dynamic_slice_in_dim(centroids, slab_index * rows, rows, 0))
    refined = (sums + PRIOR_WEIGHT * mine) / (counts[:, None] + PRIOR_WEIGHT)
    return refined, counts


def solution(mesh):
    owners, slabs = mesh.devices.shape
    split = Mesh(mesh.devices.reshape(2, owners // 4, 2, slabs), OWNER + ("slab",))
    every = OWNER + ("slab",)
    placed = (P(every, None), P(every, None), P(OWNER, None))
    return jax.shard_map(
        lambda *args: shards(*args),
        mesh=split,
        in_specs=placed,
        out_specs=(P(every, None), P(every)),
        check_vma=False,
    )
```

```python
import functools
import math

import jax
import jax.numpy as jnp
from jax import lax
from jax.experimental import pallas as pl
from jax.experimental.pallas import tpu as pltpu
from jax.sharding import Mesh
from jax.sharding import PartitionSpec as P

EMBED_WIDTH = 128
CENT_BLK = 256
TOK_BLK = 256
BPO = 32
MSG_ROWS = CENT_BLK + 8

SOFTMAX_TEMP = 0.1
PRIOR_WEIGHT = 4.0
EPSILON = 1e-06
EXP2_SCALE = math.log2(math.e) / (EMBED_WIDTH * SOFTMAX_TEMP)


def unit_rows(values):
    widened = values.astype(jnp.float32)
    return widened * lax.rsqrt(jnp.mean(widened * widened, axis=-1, keepdims=True) + EPSILON)


def split_counts(totals_a, totals_b):
    row = lax.broadcasted_iota(jnp.int32, (8, EMBED_WIDTH), 0)
    heads = jnp.where(row % 2 == 0, totals_a, totals_b)
    rounded = heads.astype(jnp.bfloat16).astype(jnp.float32)
    tails = heads - rounded
    tile = jnp.where(row < 2, rounded, jnp.where(row < 4, tails, 0.0))
    return tile.astype(jnp.bfloat16)


def prepare_kernel(tok_ref, unit_ref, turned_ref):
    tok = unit_rows(tok_ref[...]).astype(jnp.bfloat16)
    unit_ref[...] = tok
    for at in range(turned_ref.shape[0]):
        turned_ref[at] = tok[at * TOK_BLK:(at + 1) * TOK_BLK].T


def prepare(tokens, per_step=16):
    blocks = tokens.shape[0] // TOK_BLK
    per_step = math.gcd(per_step, blocks)
    rows = per_step * TOK_BLK
    return pl.pallas_call(
        prepare_kernel,
        grid=(blocks // per_step,),
        in_specs=[pl.BlockSpec((rows, EMBED_WIDTH), lambda i: (i, 0))],
        out_specs=(
            pl.BlockSpec((rows, EMBED_WIDTH), lambda i: (i, 0)),
            pl.BlockSpec((per_step, EMBED_WIDTH, TOK_BLK), lambda i: (i, 0, 0)),
        ),
        out_shape=(
            jax.ShapeDtypeStruct(tokens.shape, jnp.bfloat16),
            jax.ShapeDtypeStruct((blocks, EMBED_WIDTH, TOK_BLK), jnp.bfloat16),
        ),
        compiler_params=pltpu.CompilerParams(vmem_limit_bytes=56 << 20),
        cost_estimate=pl.CostEstimate(
            flops=tokens.size * 4, transcendentals=tokens.shape[0], bytes_accessed=tokens.size * 6
        ),
        name="prepare",
    )(tokens)


def attend_kernel(
    unroll, parts, slots, ids, zpos, unit_hbm, turned_hbm, near_ref, far_ref, out_ref,
    acc_ref, cnt_ref, exp_ref, inv_ref, cent_ref, unit_ref, turned_ref, unit_sems, turned_sems,
):
    blocks = turned_ref.shape[0]
    share = blocks // parts

    def unit_copy(part):
        rows = pl.ds(pl.multiple_of(part * share * TOK_BLK, TOK_BLK), share * TOK_BLK)
        return pltpu.make_async_copy(unit_hbm.at[rows], unit_ref.at[rows], unit_sems.at[part])

    def turned_copy(part):
        rows = pl.ds(part * share, share)
        return pltpu.make_async_copy(turned_hbm.at[rows], turned_ref.at[rows], turned_sems.at[part])

    for part in range(parts):
        unit_copy(part).start()
        turned_copy(part).start()
    acc_ref[...] = jnp.zeros_like(acc_ref)
    cnt_ref[...] = jnp.zeros_like(cnt_ref)
    exp_ref[1] = jnp.zeros(exp_ref.shape[1:], exp_ref.dtype)
    inv_ref[1] = jnp.zeros(inv_ref.shape[1:], inv_ref.dtype)
    depth = near_ref.shape[2] + far_ref.shape[2]
    cores = 2
    for first, recv_ref in ((0, near_ref), (near_ref.shape[2], far_ref)):
        def turn(quad, carry):
            for at in range(recv_ref.shape[2]):
                rows = recv_ref[quad, :, at].reshape(CENT_BLK, EMBED_WIDTH)
                slot = ((quad // cores) * depth + zpos[first + at]) * cores + quad % cores
                cent_ref[slot] = rows.T
            return carry

        lax.fori_loop(0, near_ref.shape[0], turn, 0)

    def spread(block, side):
        inverse = inv_ref[side]

        def piece(k):
            slot = slots[block * 3 + k]
            left = exp_ref[side, k, :, :128] * inverse
            right = exp_ref[side, k, :, 128:] * inverse
            weights = jnp.concatenate([left, right], axis=1)
            cnt_ref[slot] += jnp.sum(weights.reshape(TOK_BLK // 8, 8, CENT_BLK), axis=0)
            acc_ref[slot] += jnp.dot(
                turned_ref[block], weights.astype(jnp.bfloat16), preferred_element_type=jnp.float32
            )

        return piece

    def score(block, side):
        tok = unit_ref[pl.ds(pl.multiple_of(block * TOK_BLK, TOK_BLK), TOK_BLK), :]
        totals = []

        def piece(k):
            slot = slots[block * 3 + k]
            scores = jnp.dot(tok, cent_ref[slot], preferred_element_type=jnp.float32)
            grown = jnp.exp2(scores * EXP2_SCALE)
            exp_ref[side, k] = grown
            part = grown[:, :128] + grown[:, 128:]
            totals.append(part if not totals else totals.pop() + part)

        def close():
            total = jnp.sum(totals[0], axis=1, keepdims=True)
            inv_ref[side] = jnp.broadcast_to(1.0 / total, inv_ref.shape[1:])

        return piece, close

    def round_of(index, carry):
        @pl.when(index % (share // unroll) == 0)
        def _():
            unit_copy(index // (share // unroll)).wait()
            turned_copy(index // (share // unroll)).wait()

        for u in range(unroll):
            block = unroll * index + u
            piece_a, close = score(block, u % 2)
            piece_b = spread(jnp.maximum(block - 1, 0), (u + 1) % 2)
            for k in range(3):
                piece_a(k)
                piece_b(k)
            close()
        return carry

    lax.fori_loop(0, blocks // unroll, round_of, 0)
    piece = spread(blocks - 1, 1)
    for k in range(3):
        piece(k)
    finish(ids, out_ref, acc_ref, cnt_ref)


def finish(ids, out_ref, acc_ref, cnt_ref):
    row = lax.broadcasted_iota(jnp.int32, (8, EMBED_WIDTH), 0)

    def write(slot, carry):
        out_ref[slot, :128, :] = acc_ref[slot, :, :128].astype(jnp.bfloat16)
        out_ref[slot, 128:256, :] = acc_ref[slot, :, 128:].astype(jnp.bfloat16)
        counts = jnp.sum(cnt_ref[slot], axis=0, keepdims=True)
        tile = split_counts(counts[:, :128], counts[:, 128:])
        named = jnp.full(tile.shape, ids[slot].astype(jnp.float32))
        out_ref[slot, CENT_BLK:, :] = jnp.where(row == 4, named, tile.astype(jnp.float32)).astype(jnp.bfloat16)
        return carry

    lax.fori_loop(0, cnt_ref.shape[0], write, 0, unroll=4)


def attend(slots, ids, zpos, unit, turned, near, far, unroll=8):
    owners = ids.shape[0]
    blocks = turned.shape[0]
    unroll = math.gcd(unroll, blocks)
    parts = math.gcd(4, blocks // unroll)
    pairs = blocks * 3 * TOK_BLK * CENT_BLK
    whole = lambda shape: pl.BlockSpec(
        shape, lambda i, s, n, z: (0,) * len(shape), pipeline_mode=pl.Buffered(1)
    )
    shape = (owners, MSG_ROWS, EMBED_WIDTH)
    return pl.pallas_call(
        functools.partial(attend_kernel, unroll, parts),
        grid_spec=pltpu.PrefetchScalarGridSpec(
            num_scalar_prefetch=3,
            grid=(1,),
            in_specs=[
                pl.BlockSpec(memory_space=pl.ANY),
                pl.BlockSpec(memory_space=pl.ANY),
                whole(near.shape),
                whole(far.shape),
            ],
            out_specs=whole(shape),
            scratch_shapes=[
                pltpu.VMEM((owners, EMBED_WIDTH, CENT_BLK), jnp.float32),
                pltpu.VMEM((owners, 8, CENT_BLK), jnp.float32),
                pltpu.VMEM((2, 3, TOK_BLK, CENT_BLK), jnp.float32),
                pltpu.VMEM((2, TOK_BLK, 128), jnp.float32),
                pltpu.VMEM((owners, EMBED_WIDTH, CENT_BLK), jnp.bfloat16),
                pltpu.VMEM(unit.shape, jnp.bfloat16),
                pltpu.VMEM(turned.shape, jnp.bfloat16),
                pltpu.SemaphoreType.DMA((parts,)),
                pltpu.SemaphoreType.DMA((parts,)),
            ],
        ),
        out_shape=jax.ShapeDtypeStruct(shape, jnp.bfloat16),
        compiler_params=pltpu.CompilerParams(vmem_limit_bytes=48 << 20),
        cost_estimate=pl.CostEstimate(
            flops=pairs * EMBED_WIDTH * 4, transcendentals=pairs, bytes_accessed=unit.size * 6
        ),
        name="attend",
    )(slots, ids, zpos, unit, turned, near, far)


def pick_kernel(asked, zpos, depth, *refs):
    pieces, out_ref = refs[:-1], refs[-1]

    def fill(peer, carry):
        for at in range(len(pieces)):
            inner = asked[peer * depth[0] + zpos[at]]
            out_ref[peer, at] = pieces[at][jnp.maximum(inner, 0)]
        return carry

    lax.fori_loop(0, out_ref.shape[0], fill, 0, unroll=4)


def pick(asked, zpos, pieces, peers):
    rows = pieces[0].shape[1]
    shape = (peers, len(pieces), rows, EMBED_WIDTH)
    depth = jnp.full((1,), asked.shape[0] // peers, jnp.int32)
    return pl.pallas_call(
        pick_kernel,
        grid_spec=pltpu.PrefetchScalarGridSpec(
            num_scalar_prefetch=3,
            grid=(1,),
            in_specs=[
                pl.BlockSpec(p.shape, lambda i, s, n, d: (0, 0, 0), pipeline_mode=pl.Buffered(1))
                for p in pieces
            ],
            out_specs=pl.BlockSpec(
                shape, lambda i, s, n, d: (0, 0, 0, 0), pipeline_mode=pl.Buffered(1)
            ),
        ),
        out_shape=jax.ShapeDtypeStruct(shape, jnp.bfloat16),
        compiler_params=pltpu.CompilerParams(vmem_limit_bytes=8 << 20),
        cost_estimate=pl.CostEstimate(flops=0, transcendentals=0, bytes_accessed=4 << 20),
        name="pick",
    )(asked, zpos, depth, *pieces)


def gather_ring(piece, axis):
    depth = lax.axis_size(axis)
    up = [(i, (i + 1) % depth) for i in range(depth)]
    down = [(i, (i - 1) % depth) for i in range(depth)]
    pieces = {0: piece}
    rise, fall = depth // 2, (depth - 1) // 2
    for step in range(1, rise + 1):
        pieces[step] = lax.ppermute(pieces[step - 1], axis, up)
        if step <= fall:
            pieces[-step] = lax.ppermute(pieces[1 - step], axis, down)
    pieces = {away % depth: piece for away, piece in pieces.items()}
    return [pieces[k] for k in range(depth)]


def collect_kernel(asked, back_ref, out_ref, acc_ref):
    acc_ref[...] = jnp.zeros_like(acc_ref)

    def add(source, carry):
        inner = asked[source]
        sent = back_ref[source].astype(jnp.float32)
        acc_ref[jnp.maximum(inner, 0)] += jnp.where(inner >= 0, sent, 0.0)
        return carry

    lax.fori_loop(0, back_ref.shape[0], add, 0, unroll=4)

    def write(inner, carry):
        out_ref[inner, :CENT_BLK, :] = acc_ref[inner, :CENT_BLK, :].astype(jnp.bfloat16)
        tile = acc_ref[inner, CENT_BLK:, :]
        totals = tile[0:2] + tile[2:4]
        out_ref[inner, CENT_BLK:, :] = split_counts(totals[0:1], totals[1:2])
        return carry

    lax.fori_loop(0, out_ref.shape[0], write, 0, unroll=4)


def collect(asked, back):
    shape = (BPO, MSG_ROWS, EMBED_WIDTH)
    return pl.pallas_call(
        collect_kernel,
        grid_spec=pltpu.PrefetchScalarGridSpec(
            num_scalar_prefetch=1,
            grid=(1,),
            in_specs=[pl.BlockSpec(back.shape, lambda i, s: (0, 0, 0), pipeline_mode=pl.Buffered(1))],
            out_specs=pl.BlockSpec(shape, lambda i, s: (0, 0, 0), pipeline_mode=pl.Buffered(1)),
            scratch_shapes=[pltpu.VMEM(shape, jnp.float32)],
        ),
        out_shape=jax.ShapeDtypeStruct(shape, jnp.bfloat16),
        compiler_params=pltpu.CompilerParams(vmem_limit_bytes=24 << 20),
        cost_estimate=pl.CostEstimate(
            flops=back.size, transcendentals=0, bytes_accessed=back.size * 4
        ),
        name="collect",
    )(asked, back)


OWNER = ("xlo", "z", "core")
PLANE = ("xlo", "core", "slab")


def shards(tokens, listed, centroids):
    slab_count = lax.axis_size("slab")
    slab_index = lax.axis_index("slab")
    depth = lax.axis_size("z")
    cores = lax.axis_size("core")
    quads = lax.axis_size("xlo") * cores
    owner_count = quads * depth
    peers = quads * slab_count
    share_blocks = BPO // slab_count
    share_rows = CENT_BLK // slab_count

    blocks = centroids.reshape(BPO, CENT_BLK, EMBED_WIDTH)
    piece = lax.dynamic_slice_in_dim(blocks, slab_index * share_rows, share_rows, 1)
    piece = unit_rows(piece).astype(jnp.bfloat16)
    pieces = gather_ring(piece, "z")

    owner_ids = jnp.arange(owner_count, dtype=jnp.int32)
    group_of = listed // BPO
    inner_ids = listed % BPO
    matches = group_of[:, :, None] == owner_ids
    wanted = jnp.max(jnp.where(matches, inner_ids[:, :, None] + 1, 0), axis=(0, 1)) - 1
    by_quad = wanted.reshape(-1, depth, cores).transpose(0, 2, 1).reshape(quads, 1, depth)
    requests = jnp.broadcast_to(by_quad, (quads, slab_count, depth)).reshape(peers, 1, depth)
    asked = lax.all_to_all(requests, PLANE, split_axis=0, concat_axis=0, tiled=True)
    asked = asked.reshape(-1)

    tokens, _ = lax.optimization_barrier((tokens, asked))
    unit, turned = prepare(tokens)
    reach = depth // 4
    order = sorted(range(depth), key=lambda away: (min(away, depth - away), away))
    zpos = (lax.axis_index("z") - jnp.array(order, jnp.int32)) % depth
    split = 2 * reach + 1
    received = []
    for part in (slice(0, split), slice(split, depth)):
        picked = pick(asked, zpos[part], [pieces[away] for away in order[part]], peers)
        recv = lax.all_to_all(picked, PLANE, split_axis=0, concat_axis=0, tiled=True)
        received.append(recv.reshape(quads, slab_count, -1, share_rows, EMBED_WIDTH))

    partial = attend(group_of.reshape(-1), wanted, zpos, unit, turned, *received)
    back = lax.all_to_all(partial, OWNER, split_axis=0, concat_axis=0, tiled=True)
    own = collect(back[:, CENT_BLK + 4, 0].astype(jnp.int32), back)
    slabs = lax.all_to_all(own, "slab", split_axis=0, concat_axis=0, tiled=True)
    slabs = slabs.reshape(slab_count, share_blocks, MSG_ROWS, EMBED_WIDTH)

    totals = jnp.sum(slabs.astype(jnp.float32), axis=0)
    counts = (totals[:, CENT_BLK:CENT_BLK + 2] + totals[:, CENT_BLK + 2:CENT_BLK + 4]).reshape(-1)
    halves = totals[:, :CENT_BLK].reshape(share_blocks, 2, EMBED_WIDTH, CENT_BLK // 2)
    sums = halves.transpose(0, 1, 3, 2).reshape(-1, EMBED_WIDTH)
    rows = share_blocks * CENT_BLK
    mine = unit_rows(lax.dynamic_slice_in_dim(centroids, slab_index * rows, rows, 0))
    refined = (sums + PRIOR_WEIGHT * mine) / (counts[:, None] + PRIOR_WEIGHT)
    return refined, counts


def solution(mesh):
    owners, slabs = mesh.devices.shape
    split = Mesh(mesh.devices.reshape(2, owners // 4, 2, slabs), OWNER + ("slab",))
    every = OWNER + ("slab",)
    placed = (P(every, None), P(every, None), P(OWNER, None))
    return jax.shard_map(
        lambda *args: shards(*args),
        mesh=split,
        in_specs=placed,
        out_specs=(P(every, None), P(every)),
        check_vma=False,
    )
```

```python
import functools
import math

import jax
import jax.numpy as jnp
from jax import lax
from jax.experimental import pallas as pl
from jax.experimental.pallas import tpu as pltpu
from jax.sharding import Mesh
from jax.sharding import PartitionSpec as P

EMBED_WIDTH = 128
CENT_BLK = 256
TOK_BLK = 256
BPO = 32
MSG_ROWS = CENT_BLK + 8

SOFTMAX_TEMP = 0.1
PRIOR_WEIGHT = 4.0
EPSILON = 1e-06
EXP2_SCALE = math.log2(math.e) / (EMBED_WIDTH * SOFTMAX_TEMP)


def unit_rows(values):
    widened = values.astype(jnp.float32)
    return widened * lax.rsqrt(jnp.mean(widened * widened, axis=-1, keepdims=True) + EPSILON)


def split_counts(totals_a, totals_b):
    row = lax.broadcasted_iota(jnp.int32, (8, EMBED_WIDTH), 0)
    heads = jnp.where(row % 2 == 0, totals_a, totals_b)
    rounded = heads.astype(jnp.bfloat16).astype(jnp.float32)
    tails = heads - rounded
    tile = jnp.where(row < 2, rounded, jnp.where(row < 4, tails, 0.0))
    return tile.astype(jnp.bfloat16)


def prepare_kernel(tok_ref, unit_ref, turned_ref):
    tok = unit_rows(tok_ref[...]).astype(jnp.bfloat16)
    unit_ref[...] = tok
    for at in range(turned_ref.shape[0]):
        turned_ref[at] = tok[at * TOK_BLK:(at + 1) * TOK_BLK].T


def prepare(tokens, per_step=16):
    blocks = tokens.shape[0] // TOK_BLK
    per_step = math.gcd(per_step, blocks)
    rows = per_step * TOK_BLK
    return pl.pallas_call(
        prepare_kernel,
        grid=(blocks // per_step,),
        in_specs=[pl.BlockSpec((rows, EMBED_WIDTH), lambda i: (i, 0))],
        out_specs=(
            pl.BlockSpec((rows, EMBED_WIDTH), lambda i: (i, 0)),
            pl.BlockSpec((per_step, EMBED_WIDTH, TOK_BLK), lambda i: (i, 0, 0)),
        ),
        out_shape=(
            jax.ShapeDtypeStruct(tokens.shape, jnp.bfloat16),
            jax.ShapeDtypeStruct((blocks, EMBED_WIDTH, TOK_BLK), jnp.bfloat16),
        ),
        compiler_params=pltpu.CompilerParams(vmem_limit_bytes=56 << 20),
        cost_estimate=pl.CostEstimate(
            flops=tokens.size * 4, transcendentals=tokens.shape[0], bytes_accessed=tokens.size * 6
        ),
        name="prepare",
    )(tokens)


def attend_kernel(
    unroll, parts, slots, ids, zpos, unit_hbm, turned_hbm, near_ref, far_ref, out_ref,
    acc_ref, cnt_ref, exp_ref, inv_ref, cent_ref, unit_ref, turned_ref, unit_sems, turned_sems,
):
    blocks = turned_ref.shape[0]
    share = blocks // parts

    def unit_copy(part):
        rows = pl.ds(pl.multiple_of(part * share * TOK_BLK, TOK_BLK), share * TOK_BLK)
        return pltpu.make_async_copy(unit_hbm.at[rows], unit_ref.at[rows], unit_sems.at[part])

    def turned_copy(part):
        rows = pl.ds(part * share, share)
        return pltpu.make_async_copy(turned_hbm.at[rows], turned_ref.at[rows], turned_sems.at[part])

    for part in range(parts):
        unit_copy(part).start()
        turned_copy(part).start()
    acc_ref[...] = jnp.zeros_like(acc_ref)
    cnt_ref[...] = jnp.zeros_like(cnt_ref)
    exp_ref[1] = jnp.zeros(exp_ref.shape[1:], exp_ref.dtype)
    inv_ref[1] = jnp.zeros(inv_ref.shape[1:], inv_ref.dtype)
    reach = near_ref.shape[1]
    depth = reach + far_ref.shape[2]
    cores = 2

    def place(quad, carry):
        first = (quad // cores) * depth
        for at in range(depth):
            slot = (first + zpos[at]) * cores + quad % cores
            if at < reach:
                cent_ref[slot] = near_ref[quad, at]
            else:
                cent_ref[slot] = far_ref[quad, :, at - reach].reshape(CENT_BLK, EMBED_WIDTH).T
        return carry

    lax.fori_loop(0, near_ref.shape[0], place, 0)

    def spread(block, side):
        inverse = inv_ref[side]

        def piece(k):
            slot = slots[block * 3 + k]
            left = exp_ref[side, k, :, :128] * inverse
            right = exp_ref[side, k, :, 128:] * inverse
            weights = jnp.concatenate([left, right], axis=1)
            cnt_ref[slot] += jnp.sum(weights.reshape(TOK_BLK // 8, 8, CENT_BLK), axis=0)
            acc_ref[slot] += jnp.dot(
                turned_ref[block], weights.astype(jnp.bfloat16), preferred_element_type=jnp.float32
            )

        return piece

    def score(block, side):
        tok = unit_ref[pl.ds(pl.multiple_of(block * TOK_BLK, TOK_BLK), TOK_BLK), :]
        totals = []

        def piece(k):
            slot = slots[block * 3 + k]
            scores = jnp.dot(tok, cent_ref[slot], preferred_element_type=jnp.float32)
            grown = jnp.exp2(scores * EXP2_SCALE)
            exp_ref[side, k] = grown
            part = grown[:, :128] + grown[:, 128:]
            totals.append(part if not totals else totals.pop() + part)

        def close():
            total = jnp.sum(totals[0], axis=1, keepdims=True)
            inv_ref[side] = jnp.broadcast_to(1.0 / total, inv_ref.shape[1:])

        return piece, close

    def round_of(index, carry):
        @pl.when(index % (share // unroll) == 0)
        def _():
            unit_copy(index // (share // unroll)).wait()
            turned_copy(index // (share // unroll)).wait()

        for u in range(unroll):
            block = unroll * index + u
            piece_a, close = score(block, u % 2)
            piece_b = spread(jnp.maximum(block - 1, 0), (u + 1) % 2)
            for k in range(3):
                piece_a(k)
                piece_b(k)
            close()
        return carry

    lax.fori_loop(0, blocks // unroll, round_of, 0)
    piece = spread(blocks - 1, 1)
    for k in range(3):
        piece(k)
    finish(ids, out_ref, acc_ref, cnt_ref)


def finish(ids, out_ref, acc_ref, cnt_ref):
    row = lax.broadcasted_iota(jnp.int32, (8, EMBED_WIDTH), 0)

    def write(slot, carry):
        out_ref[slot, :128, :] = acc_ref[slot, :, :128].astype(jnp.bfloat16)
        out_ref[slot, 128:256, :] = acc_ref[slot, :, 128:].astype(jnp.bfloat16)
        counts = jnp.sum(cnt_ref[slot], axis=0, keepdims=True)
        tile = split_counts(counts[:, :128], counts[:, 128:])
        named = jnp.full(tile.shape, ids[slot].astype(jnp.float32))
        out_ref[slot, CENT_BLK:, :] = jnp.where(row == 4, named, tile.astype(jnp.float32)).astype(jnp.bfloat16)
        return carry

    lax.fori_loop(0, cnt_ref.shape[0], write, 0, unroll=4)


def attend(slots, ids, zpos, unit, turned, near, far, unroll=8):
    owners = ids.shape[0]
    blocks = turned.shape[0]
    unroll = math.gcd(unroll, blocks)
    parts = math.gcd(4, blocks // unroll)
    pairs = blocks * 3 * TOK_BLK * CENT_BLK
    whole = lambda shape: pl.BlockSpec(
        shape, lambda i, s, n, z: (0,) * len(shape), pipeline_mode=pl.Buffered(1)
    )
    shape = (owners, MSG_ROWS, EMBED_WIDTH)
    return pl.pallas_call(
        functools.partial(attend_kernel, unroll, parts),
        grid_spec=pltpu.PrefetchScalarGridSpec(
            num_scalar_prefetch=3,
            grid=(1,),
            in_specs=[
                pl.BlockSpec(memory_space=pl.ANY),
                pl.BlockSpec(memory_space=pl.ANY),
                whole(near.shape),
                whole(far.shape),
            ],
            out_specs=whole(shape),
            scratch_shapes=[
                pltpu.VMEM((owners, EMBED_WIDTH, CENT_BLK), jnp.float32),
                pltpu.VMEM((owners, 8, CENT_BLK), jnp.float32),
                pltpu.VMEM((2, 3, TOK_BLK, CENT_BLK), jnp.float32),
                pltpu.VMEM((2, TOK_BLK, 128), jnp.float32),
                pltpu.VMEM((owners, EMBED_WIDTH, CENT_BLK), jnp.bfloat16),
                pltpu.VMEM(unit.shape, jnp.bfloat16),
                pltpu.VMEM(turned.shape, jnp.bfloat16),
                pltpu.SemaphoreType.DMA((parts,)),
                pltpu.SemaphoreType.DMA((parts,)),
            ],
        ),
        out_shape=jax.ShapeDtypeStruct(shape, jnp.bfloat16),
        compiler_params=pltpu.CompilerParams(vmem_limit_bytes=48 << 20),
        cost_estimate=pl.CostEstimate(
            flops=pairs * EMBED_WIDTH * 4, transcendentals=pairs, bytes_accessed=unit.size * 6
        ),
        name="attend",
    )(slots, ids, zpos, unit, turned, near, far)


def turn_kernel(recv_ref, out_ref):
    def turn(quad, carry):
        for at in range(out_ref.shape[1]):
            out_ref[quad, at] = recv_ref[quad, :, at].reshape(CENT_BLK, EMBED_WIDTH).T
        return carry

    lax.fori_loop(0, out_ref.shape[0], turn, 0)


def turn_blocks(recv):
    shape = (recv.shape[0], recv.shape[2], EMBED_WIDTH, CENT_BLK)
    return pl.pallas_call(
        turn_kernel,
        out_shape=jax.ShapeDtypeStruct(shape, jnp.bfloat16),
        in_specs=[pl.BlockSpec(memory_space=pltpu.VMEM)],
        out_specs=pl.BlockSpec(memory_space=pltpu.VMEM),
        compiler_params=pltpu.CompilerParams(vmem_limit_bytes=8 << 20),
        cost_estimate=pl.CostEstimate(flops=0, transcendentals=0, bytes_accessed=recv.size * 4),
        name="turn",
    )(recv)


def pick_kernel(asked, zpos, depth, *refs):
    pieces, out_ref = refs[:-1], refs[-1]

    def fill(peer, carry):
        for at in range(len(pieces)):
            inner = asked[peer * depth[0] + zpos[at]]
            out_ref[peer, at] = pieces[at][jnp.maximum(inner, 0)]
        return carry

    lax.fori_loop(0, out_ref.shape[0], fill, 0, unroll=4)


def pick(asked, zpos, pieces, peers):
    rows = pieces[0].shape[1]
    shape = (peers, len(pieces), rows, EMBED_WIDTH)
    depth = jnp.full((1,), asked.shape[0] // peers, jnp.int32)
    return pl.pallas_call(
        pick_kernel,
        grid_spec=pltpu.PrefetchScalarGridSpec(
            num_scalar_prefetch=3,
            grid=(1,),
            in_specs=[
                pl.BlockSpec(p.shape, lambda i, s, n, d: (0, 0, 0), pipeline_mode=pl.Buffered(1))
                for p in pieces
            ],
            out_specs=pl.BlockSpec(
                shape, lambda i, s, n, d: (0, 0, 0, 0), pipeline_mode=pl.Buffered(1)
            ),
        ),
        out_shape=jax.ShapeDtypeStruct(shape, jnp.bfloat16),
        compiler_params=pltpu.CompilerParams(vmem_limit_bytes=8 << 20),
        cost_estimate=pl.CostEstimate(flops=0, transcendentals=0, bytes_accessed=4 << 20),
        name="pick",
    )(asked, zpos, depth, *pieces)


def gather_ring(piece, axis):
    depth = lax.axis_size(axis)
    up = [(i, (i + 1) % depth) for i in range(depth)]
    down = [(i, (i - 1) % depth) for i in range(depth)]
    pieces = {0: piece}
    rise, fall = depth // 2, (depth - 1) // 2
    for step in range(1, rise + 1):
        pieces[step] = lax.ppermute(pieces[step - 1], axis, up)
        if step <= fall:
            pieces[-step] = lax.ppermute(pieces[1 - step], axis, down)
    pieces = {away % depth: piece for away, piece in pieces.items()}
    return [pieces[k] for k in range(depth)]


def collect_kernel(asked, back_ref, out_ref, acc_ref):
    acc_ref[...] = jnp.zeros_like(acc_ref)

    def add(source, carry):
        inner = asked[source]
        sent = back_ref[source].astype(jnp.float32)
        acc_ref[jnp.maximum(inner, 0)] += jnp.where(inner >= 0, sent, 0.0)
        return carry

    lax.fori_loop(0, back_ref.shape[0], add, 0, unroll=4)

    def write(inner, carry):
        out_ref[inner, :CENT_BLK, :] = acc_ref[inner, :CENT_BLK, :].astype(jnp.bfloat16)
        tile = acc_ref[inner, CENT_BLK:, :]
        totals = tile[0:2] + tile[2:4]
        out_ref[inner, CENT_BLK:, :] = split_counts(totals[0:1], totals[1:2])
        return carry

    lax.fori_loop(0, out_ref.shape[0], write, 0, unroll=4)


def collect(asked, back):
    shape = (BPO, MSG_ROWS, EMBED_WIDTH)
    return pl.pallas_call(
        collect_kernel,
        grid_spec=pltpu.PrefetchScalarGridSpec(
            num_scalar_prefetch=1,
            grid=(1,),
            in_specs=[pl.BlockSpec(back.shape, lambda i, s: (0, 0, 0), pipeline_mode=pl.Buffered(1))],
            out_specs=pl.BlockSpec(shape, lambda i, s: (0, 0, 0), pipeline_mode=pl.Buffered(1)),
            scratch_shapes=[pltpu.VMEM(shape, jnp.float32)],
        ),
        out_shape=jax.ShapeDtypeStruct(shape, jnp.bfloat16),
        compiler_params=pltpu.CompilerParams(vmem_limit_bytes=24 << 20),
        cost_estimate=pl.CostEstimate(
            flops=back.size, transcendentals=0, bytes_accessed=back.size * 4
        ),
        name="collect",
    )(asked, back)


OWNER = ("xlo", "z", "core")
PLANE = ("xlo", "core", "slab")


def shards(tokens, listed, centroids):
    slab_count = lax.axis_size("slab")
    slab_index = lax.axis_index("slab")
    depth = lax.axis_size("z")
    cores = lax.axis_size("core")
    quads = lax.axis_size("xlo") * cores
    owner_count = quads * depth
    peers = quads * slab_count
    share_blocks = BPO // slab_count
    share_rows = CENT_BLK // slab_count

    blocks = centroids.reshape(BPO, CENT_BLK, EMBED_WIDTH)
    piece = lax.dynamic_slice_in_dim(blocks, slab_index * share_rows, share_rows, 1)
    piece = unit_rows(piece).astype(jnp.bfloat16)
    pieces = gather_ring(piece, "z")

    owner_ids = jnp.arange(owner_count, dtype=jnp.int32)
    group_of = listed // BPO
    inner_ids = listed % BPO
    matches = group_of[:, :, None] == owner_ids
    wanted = jnp.max(jnp.where(matches, inner_ids[:, :, None] + 1, 0), axis=(0, 1)) - 1
    by_quad = wanted.reshape(-1, depth, cores).transpose(0, 2, 1).reshape(quads, 1, depth)
    requests = jnp.broadcast_to(by_quad, (quads, slab_count, depth)).reshape(peers, 1, depth)
    asked = lax.all_to_all(requests, PLANE, split_axis=0, concat_axis=0, tiled=True)
    asked = asked.reshape(-1)

    tokens, _ = lax.optimization_barrier((tokens, asked))
    unit, turned = prepare(tokens)
    reach = depth // 4
    order = sorted(range(depth), key=lambda away: (min(away, depth - away), away))
    zpos = (lax.axis_index("z") - jnp.array(order, jnp.int32)) % depth
    split = 2 * reach + 1
    received = []
    for part in (slice(0, split), slice(split, depth)):
        picked = pick(asked, zpos[part], [pieces[away] for away in order[part]], peers)
        recv = lax.all_to_all(picked, PLANE, split_axis=0, concat_axis=0, tiled=True)
        received.append(recv.reshape(quads, slab_count, -1, share_rows, EMBED_WIDTH))

    near, far = received
    partial = attend(group_of.reshape(-1), wanted, zpos, unit, turned, turn_blocks(near), far)
    back = lax.all_to_all(partial, OWNER, split_axis=0, concat_axis=0, tiled=True)
    own = collect(back[:, CENT_BLK + 4, 0].astype(jnp.int32), back)
    slabs = lax.all_to_all(own, "slab", split_axis=0, concat_axis=0, tiled=True)
    slabs = slabs.reshape(slab_count, share_blocks, MSG_ROWS, EMBED_WIDTH)

    totals = jnp.sum(slabs.astype(jnp.float32), axis=0)
    counts = (totals[:, CENT_BLK:CENT_BLK + 2] + totals[:, CENT_BLK + 2:CENT_BLK + 4]).reshape(-1)
    halves = totals[:, :CENT_BLK].reshape(share_blocks, 2, EMBED_WIDTH, CENT_BLK // 2)
    sums = halves.transpose(0, 1, 3, 2).reshape(-1, EMBED_WIDTH)
    rows = share_blocks * CENT_BLK
    mine = unit_rows(lax.dynamic_slice_in_dim(centroids, slab_index * rows, rows, 0))
    refined = (sums + PRIOR_WEIGHT * mine) / (counts[:, None] + PRIOR_WEIGHT)
    return refined, counts


def solution(mesh):
    owners, slabs = mesh.devices.shape
    split = Mesh(mesh.devices.reshape(2, owners // 4, 2, slabs), OWNER + ("slab",))
    every = OWNER + ("slab",)
    placed = (P(every, None), P(every, None), P(OWNER, None))
    return jax.shard_map(
        lambda *args: shards(*args),
        mesh=split,
        in_specs=placed,
        out_specs=(P(every, None), P(every)),
        check_vma=False,
    )
```
